128 devices in a mesh: vocab: 16 (over z, x), width: 8 (over y, core).
Axes of the slice: x: 4, y: 4, z: 4, core: 2. Of those that a mesh axis runs over, the one named last changes fastest.
Arguments:
- hidden: bfloat16 [16384, 1024], P('vocab', 'width'), may hold values from -60 to 60
- norm_gain: float32 [1024], P('width'), may hold values from 0.5 to 1.5
- head_weight: bfloat16 [1024, 32128], P('width', 'vocab'), may hold values from -1 to 1
- token_ids: int32 [16384], P('width'), may hold values from 0 to 32127
- seq_lengths: int32 [8], replicated, may hold values from 1 to 2048, as said below
Outputs:
- log_probs: float32 [16384], P('width')
- entropies: float32 [16384], P('width')
The draws below stay inside these ranges and needn't reach their ends.
Inputs may be any that keep to these rules, and one draw needn't show every extreme that they name: `seq_lengths`: each sequence has 1 to 2048 live tokens at its start; some sequence has exactly 2048.
All inputs are finite; a program needn't handle non-finite values.
Results may differ from the reference program's by a relative error of at most 0.0041.
Values may be sent and summed in bfloat16 or wider, within the bound.
A program may use at most 320 MiB of HBM per device.

```python
import math
import jax
import jax.numpy as jnp
from jax import lax

D = 1024
V = 32128
TOK_DEV = 1024
TOKENS = 16384
SEQ_LEN = 2048
SEQS = 8


def draw_hidden(key, part):
    key_main, key_rows, key_cols = jax.random.split(jax.random.fold_in(key, 1), 3)
    row_scale = jnp.exp(jax.random.uniform(key_rows, (TOKENS, 1), jnp.float32, 0.0, math.log(10.0)))
    col_scale = jnp.exp(jax.random.uniform(key_cols, (1, D), jnp.float32, math.log(0.5), math.log(2.0)))
    values = jnp.clip(jax.random.normal(key_main, (TOKENS, D), jnp.float32), -3.0, 3.0)
    values = values * row_scale * col_scale
    return values.astype(jnp.bfloat16)


def draw_head_weight(key, part):
    key_main = jax.random.fold_in(key, 2)
    values = jnp.clip(jax.random.normal(key_main, (D, V), jnp.float32) * 0.09375, -0.56, 0.56)
    return values.astype(jnp.bfloat16)


def draw_seq_lengths(key, part):
    key_len, key_pick = jax.random.split(jax.random.fold_in(key, 3))
    lengths = jax.random.randint(key_len, (SEQS,), 1, SEQ_LEN + 1)
    picked = jax.random.randint(key_pick, (), 0, SEQS)
    return jnp.where(jnp.arange(SEQS) == picked, SEQ_LEN, lengths).astype(jnp.int32)


def place_ends(values, rng, least, high):
    place = [jax.random.randint(jax.random.fold_in(rng, axis), (), 0, length) for axis, length in enumerate(values.shape)]
    main_axis = values.shape.index(max(values.shape))
    neighbour = place[:main_axis] + [(place[main_axis] + 1) % values.shape[main_axis]] + place[main_axis + 1:]
    return values.at[tuple(place)].set(least).at[tuple(neighbour)].set(high)


def setup_inputs(seed: int = 0) -> dict:
    keys = jax.random.split(jax.random.key(seed), 6)
    return {
        "hidden": draw_hidden(jax.random.fold_in(keys[5], 71), 0),
        "norm_gain": jnp.clip(1.0 + 0.1 * jax.random.normal(keys[1], (D,), jnp.float32), 0.5, 1.5),
        "head_weight": draw_head_weight(jax.random.fold_in(keys[5], 71), 0),
        "token_ids": place_ends(jax.random.randint(keys[3], (TOKENS,), 0, V), jax.random.fold_in(keys[3], 1), 0, V - 1).astype(jnp.int32),
        "seq_lengths": draw_seq_lengths(jax.random.fold_in(keys[5], 71), 0),
    }


def reference(hidden, norm_gain, head_weight, token_ids, seq_lengths):
    hidden_wide = hidden.astype(jnp.float32)
    mean_square = lax.optimization_barrier(jnp.mean(hidden_wide * hidden_wide, axis=1, keepdims=True))
    normed = (hidden_wide * lax.rsqrt(mean_square + 1e-06) * norm_gain[None, :]).astype(jnp.bfloat16)
    row_index = jnp.arange(TOKENS, dtype=jnp.int32)
    position = row_index % SEQ_LEN
    sequence = row_index // SEQ_LEN
    live_rows = position < seq_lengths[sequence]
    block_rows = normed.reshape(TOKENS // TOK_DEV, TOK_DEV, D)
    block_ids = token_ids.reshape(TOKENS // TOK_DEV, TOK_DEV)

    def block_stats(inputs):
        rows_here, ids_here = inputs
        logits = jnp.dot(rows_here, head_weight, preferred_element_type=jnp.float32)
        largest = lax.optimization_barrier(jnp.max(logits, axis=1, keepdims=True))
        exponent_terms = jnp.exp(logits - largest)
        total_exp = lax.optimization_barrier(jnp.sum(exponent_terms, axis=1))
        log_total = largest[:, 0] + jnp.log(total_exp)
        mean_logit = lax.optimization_barrier(jnp.sum(exponent_terms * logits, axis=1)) / total_exp
        target = jnp.take_along_axis(logits, ids_here[:, None], axis=1)[:, 0]
        return (target - log_total, log_total - mean_logit)
    log_probs, entropies = lax.map(block_stats, (block_rows, block_ids))
    log_probs = jnp.where(live_rows, log_probs.reshape(TOKENS), 0.0)
    entropies = jnp.where(live_rows, entropies.reshape(TOKENS), 0.0)
    return (log_probs, entropies)
```

```python
import jax
import jax.numpy as jnp
from jax import lax
from jax.experimental import pallas as pl
from jax.experimental.pallas import tpu as pltpu
from jax.sharding import PartitionSpec as P

D = 1024
SEQ_LEN = 2048
SIDE = 4
GROUPS = 8
ROWS = 128
CHUNK = 512
NCHUNK = 4
TILE = 256
NEG = -1e30
MESH = pl.DeviceIdType.MESH
ORDER = [(0, 0), (0, 1), (0, 3), (1, 0), (3, 0), (1, 1), (1, 3), (3, 1), (3, 3),
         (0, 2), (2, 0), (1, 2), (3, 2), (2, 1), (2, 3), (2, 2)]
SLOT = {d: i for i, d in enumerate(ORDER)}
NTILE = 16 * ROWS // TILE
STEPS = [(p, j) for p in range(NTILE) for j in range(NCHUNK)]


def kernel(hid, head, gain, ids, lens, lp_ref, ent_ref,
           xin, xn, wb, hall, hlast, gb, idb, idl, m, s, u, t, lb0, lb1, st_tx, st_rx, o_tx, o_rx,
           as_, ar, gs, gr, is_, ir, xs, xr, ws, wr, wl, ss_, sr, os_, or_):
    v = lax.axis_index("vocab")
    w = lax.axis_index("width")
    z, x = v // SIDE, v % SIDE
    y, c = w // 2, w % 2
    columns = head.shape[1]

    def at(dz, dx):
        return (lax.rem(z + dz + SIDE, SIDE) * SIDE + lax.rem(x + dx + SIDE, SIDE), w)

    def up(dy, other=0):
        return (v, lax.rem(y + dy + SIDE, SIDE) * 2 + (1 - c if other else c))

    def group(d):
        return lax.rem(w + d, GROUPS)

    def remote(src, dst, send, recv, dev):
        return pltpu.make_async_remote_copy(src_ref=src, dst_ref=dst, send_sem=send, recv_sem=recv,
                                            device_id=dev, device_id_type=MESH)

    barrier = pltpu.get_barrier_semaphore()
    peers = [(v, group(d)) for d in range(1, GROUPS)] + [at(0, 1), at(0, -1), at(1, 0), at(-1, 0)]
    for dev in peers:
        pl.semaphore_signal(barrier, inc=1, device_id=dev, device_id_type=MESH)
    pl.semaphore_wait(barrier, len(peers))

    sent = []

    def go(copy):
        copy.start()
        sent.append(copy)

    a_copies, g_copies, i_copies = [], [], []
    for d in (2, 3, 4, 5, 6, 7, 1):
        g = group(d)
        rows = pl.ds(pl.multiple_of(g * ROWS, ROWS), ROWS)
        a_copies.append(remote(hid.at[rows, :], xin.at[w], as_.at[d], ar.at[d], (v, g)))
        g_copies.append(remote(gain, gb.at[w], gs.at[d], gr.at[d], (v, g)))
        i_copies.append(remote(ids.at[:, g], idb.at[w], is_.at[d], ir.at[d], (v, g)))
    own_rows = pl.ds(pl.multiple_of(w * ROWS, ROWS), ROWS)
    local = [pltpu.make_async_copy(hid.at[own_rows, :], xin.at[w], as_.at[0]),
             pltpu.make_async_copy(gain, gb.at[w], gs.at[0]),
             pltpu.make_async_copy(ids.at[:, w], idb.at[w], is_.at[0])]
    for copy in a_copies + g_copies + i_copies:
        go(copy)
    for copy in local:
        copy.start()
    whole = pltpu.make_async_copy(head, hall, wl.at[NCHUNK])
    whole.start()

    def wrows(dy, lo=0, n=ROWS):
        src = lax.rem(y - dy + SIDE, SIDE) * 2 + c
        return pl.ds(pl.multiple_of(src * ROWS + lo, 64), n)

    W = {}
    wlocal = {}
    for j in range(NCHUNK):
        mine = head.at[:, pl.ds(j * CHUNK, CHUNK)] if j < NCHUNK - 1 else hlast

        def wv(rows):
            return wb.at[j, rows, :]

        def wcopy(k, src, dst, dev):
            W[j, k] = remote(src, dst, ws.at[j * 9 + k], wr.at[j * 9 + k], dev)

        wcopy(0, mine, wv(wrows(0)), up(1))
        wcopy(1, mine, wv(wrows(0)), up(-1))
        wcopy(2, mine, wv(wrows(0)), up(0, 1))
        wcopy(3, wv(wrows(1, 0, 64)), wv(wrows(1, 0, 64)), up(1))
        wcopy(4, wv(wrows(1)), wv(wrows(1)), up(0, 1))
        wcopy(5, wv(wrows(3, 64, 64)), wv(wrows(3, 64, 64)), up(-1))
        wcopy(6, wv(wrows(3)), wv(wrows(3)), up(0, 1))
        wcopy(7, wv(wrows(2, 0, 64)), wv(wrows(2, 0, 64)), up(0, 1))
        wcopy(8, wv(wrows(2, 64, 64)), wv(wrows(2, 64, 64)), up(0, 1))
        wlocal[j] = pltpu.make_async_copy(mine, wv(wrows(0)), wl.at[j])

    def w_own(j):
        wlocal[j].start()
        for k in (0, 1, 2):
            go(W[j, k])

    def w_forward(j):
        W[j, 0].wait_recv()
        go(W[j, 3])
        go(W[j, 4])
        W[j, 1].wait_recv()
        go(W[j, 5])
        go(W[j, 6])

    def w_across(j):
        W[j, 3].wait_recv()
        go(W[j, 7])
        W[j, 5].wait_recv()
        go(W[j, 8])

    def w_done(j):
        wlocal[j].wait()
        for k in (2, 4, 6, 7, 8):
            W[j, k].wait_recv()

    X = {}

    def xcopy(name, d, lo, n, az, ax):
        to = ((d[0] + az) % SIDE, (d[1] + ax) % SIDE)
        k = len(X)
        X[name] = remote(xn.at[SLOT[d], pl.ds(lo, n), :], xn.at[SLOT[to], pl.ds(lo, n), :],
                         xs.at[k], xr.at[k], at(az, ax))

    def turn(h, a, b):
        return (b, a) if h == 0 else (a, b)

    for h in (0, 1):
        lo = 64 * h
        for sgn, near in ((1, 1), (-1, 3)):
            q = lo if sgn == 1 else lo + 32
            xcopy((h, "first", near), (0, 0), lo, 64, *turn(h, sgn, 0))
            xcopy((h, "first", 2, near), turn(h, near, 0), q, 32, *turn(h, sgn, 0))
            for far in range(SIDE):
                xcopy((h, "second", far, near), turn(h, far, 0), lo, 64, *turn(h, 0, sgn))
                xcopy((h, "last", far, near), turn(h, far, near), q, 32, *turn(h, 0, sgn))

    def x_own():
        for h in (0, 1):
            for near in (1, 3):
                go(X[h, "first", near])
        for h in (0, 1):
            for near in (1, 3):
                go(X[h, "second", 0, near])

    def x_round1():
        for h in (0, 1):
            for near in (1, 3):
                X[h, "first", near].wait_recv()
                go(X[h, "first", 2, near])
                for side in (1, 3):
                    go(X[h, "second", near, side])

    def x_round2():
        for h in (0, 1):
            for near in (1, 3):
                X[h, "second", 0, near].wait_recv()
                go(X[h, "last", 0, near])

    def x_round3():
        for h in (0, 1):
            for near in (1, 3):
                X[h, "first", 2, near].wait_recv()
            for side in (1, 3):
                go(X[h, "second", 2, side])

    def x_round4():
        for h in (0, 1):
            for far in (1, 3):
                for near in (1, 3):
                    X[h, "second", far, near].wait_recv()
                    go(X[h, "last", far, near])

    def x_round5():
        for h in (0, 1):
            for near in (1, 3):
                X[h, "second", 2, near].wait_recv()
                go(X[h, "last", 2, near])

    def x_tail():
        for h in (0, 1):
            for far in range(SIDE):
                for near in (1, 3):
                    X[h, "last", far, near].wait_recv()

    w_own(0)
    w_own(1)

    m[...] = jnp.full(m.shape, NEG, jnp.float32)
    for ref in (s, u, t):
        ref[...] = jnp.zeros(ref.shape, jnp.float32)

    for copy in local[:2]:
        copy.wait()
    for copy in a_copies + g_copies:
        copy.wait_recv()
    for r in range(0, ROWS, 32):
        wide = [xin[k, r:r + 32, :].astype(jnp.float32) for k in range(GROUPS)]
        squares = wide[0] * wide[0]
        for k in range(1, GROUPS):
            squares = squares + wide[k] * wide[k]
        scale = lax.rsqrt(jnp.sum(squares, axis=1, keepdims=True) / D + 1e-06)
        for k in range(GROUPS):
            xn[0, r:r + 32, k * 128:(k + 1) * 128] = (wide[k] * scale * gb[k]).astype(jnp.bfloat16)
    x_own()

    whole.wait()
    first = (NCHUNK - 1) * CHUNK
    hlast[:, (columns - first) // 128 * 128:] = jnp.zeros((ROWS, CHUNK - (columns - first) // 128 * 128), jnp.bfloat16)
    hlast[:, 0:columns - first] = hall[:, first:columns]

    local[2].wait()
    for copy in i_copies:
        copy.wait_recv()
    lane = lax.broadcasted_iota(jnp.int32, (ROWS, 128), 1)
    base = v * columns
    for q, (dz, dx) in enumerate(ORDER):
        block = lax.rem(z - dz + SIDE, SIDE) * SIDE + lax.rem(x - dx + SIDE, SIDE)
        row = idb[block // 2, block % 2]
        row = jnp.where(row - base < columns, row - base, -1)
        idl[q * ROWS:(q + 1) * ROWS, :] = jnp.broadcast_to(row, (ROWS, 128)).T - lane

    w_forward(0)
    w_own(2)
    x_round1()
    w_across(0)
    w_forward(1)
    w_own(3)
    x_round2()
    x_round3()
    w_across(1)
    w_forward(2)
    x_round4()
    w_across(2)
    w_forward(3)
    x_round5()
    w_across(3)
    for j in range(NCHUNK):
        w_done(j)
    x_tail()

    def pick(values, i):
        out = jnp.int32(values[0])
        for k in range(1, len(values)):
            out = jnp.where(i >= k, jnp.int32(values[k]), out)
        return out

    def tile_of(i):
        return i // NCHUNK, i % NCHUNK

    def dot(i, buf):
        p, j = tile_of(i)
        lhs = jnp.concatenate([xn[p * 2], xn[p * 2 + 1]], axis=0)
        buf[...] = jnp.dot(lhs, wb[j], preferred_element_type=jnp.float32)

    group_rows = 16
    parts = CHUNK // 128
    lane_g = lax.broadcasted_iota(jnp.int32, (group_rows, 128), 1)

    def stats(i, buf):
        p, j = tile_of(i)
        row0 = p * TILE
        col0 = j * CHUNK
        edge = lane_g < columns - (parts - 1) * 128 - col0
        for g in range(TILE // group_rows):
            rows = pl.ds(pl.multiple_of(row0 + g * group_rows, group_rows), group_rows)
            ls = [buf[g * group_rows:(g + 1) * group_rows, k * 128:(k + 1) * 128] for k in range(parts)]
            ls[-1] = jnp.where(edge, ls[-1], NEG)
            m_old = m[rows, :]
            top = jnp.maximum(jnp.maximum(ls[0], ls[1]), jnp.maximum(ls[2], ls[3]))
            m_new = jnp.maximum(m_old, top)
            fade = jnp.exp(m_old - m_new)
            s_new = s[rows, :] * fade
            u_new = u[rows, :] * fade
            t_new = t[rows, :]
            here = idl[rows, :]
            for k in range(parts):
                e = jnp.exp(ls[k] - m_new)
                s_new = s_new + e
                u_new = u_new + e * ls[k]
                t_new = jnp.where(here == col0 + k * 128, ls[k], t_new)
            m[rows, :] = m_new
            s[rows, :] = s_new
            u[rows, :] = u_new
            t[rows, :] = t_new

    total = len(STEPS)
    dot(0, lb0)

    @pl.loop(0, total // 2)
    def _(h):
        i = h * 2
        dot(i + 1, lb1)
        stats(i, lb0)
        dot(jnp.minimum(i + 2, total - 1), lb0)
        stats(i + 1, lb1)

    @pl.loop(0, 16)
    def _(q):
        rows = pl.ds(pl.multiple_of(q * ROWS, ROWS), ROWS)
        mt = m[rows, :].T
        peak = jnp.max(mt, axis=0, keepdims=True)
        scale = jnp.exp(mt - peak)
        st_tx[q, 0:1, :] = peak
        st_tx[q, 1:2, :] = jnp.sum(s[rows, :].T * scale, axis=0, keepdims=True)
        st_tx[q, 2:3, :] = jnp.sum(u[rows, :].T * scale, axis=0, keepdims=True)
        st_tx[q, 3:4, :] = jnp.sum(t[rows, :].T, axis=0, keepdims=True)

    S = []
    for q in range(1, 16):
        dz, dx = ORDER[q]
        S.append(remote(st_tx.at[q], st_rx.at[q], ss_.at[q], sr.at[q], at(-dz, -dx)))
        go(S[-1])
    for copy in S:
        copy.wait_recv()

    stat = [st_tx[0]] + [st_rx[q] for q in range(1, 16)]
    peak = stat[0][0:1, :]
    for a in stat[1:]:
        peak = jnp.maximum(peak, a[0:1, :])
    sum_e = jnp.zeros_like(peak)
    sum_w = jnp.zeros_like(peak)
    target = jnp.zeros_like(peak)
    for a in stat:
        f = jnp.exp(a[0:1, :] - peak)
        sum_e = sum_e + a[1:2, :] * f
        sum_w = sum_w + a[2:3, :] * f
        target = target + a[3:4, :]
    log_total = peak + jnp.log(sum_e)
    position = lax.rem(v, 2) * (SEQ_LEN // 2) + w * ROWS + lax.broadcasted_iota(jnp.int32, (1, 128), 1)
    live = position < lens[v // 2]
    o_tx[0:1, :] = jnp.where(live, target - log_total, 0.0)
    o_tx[1:2, :] = jnp.where(live, log_total - sum_w / sum_e, 0.0)

    goal = v // 2
    mine = lax.rem(v, 2) * GROUPS + w
    for k in range(16):
        copy = remote(o_tx, o_rx.at[mine], os_.at[k], or_.at[mine], (k, goal))

        @pl.when(jnp.logical_not(jnp.logical_and(k == v, goal == w)))
        def _():
            copy.start()

    @pl.when(goal == w)
    def _():
        o_rx[mine] = o_tx[...]

    for k in range(16):
        copy = remote(o_tx, o_rx.at[k], os_.at[k], or_.at[k], (v, w))

        @pl.when(jnp.logical_not(jnp.logical_and(2 * w + k // GROUPS == v, k % GROUPS == w)))
        def _():
            copy.wait_recv()

        @pl.when(jnp.logical_not(jnp.logical_and(k == v, goal == w)))
        def _():
            copy.wait_send()

    for k in range(16):
        lp_ref[k:k + 1, :] = o_rx[k, 0:1, :]
        ent_ref[k:k + 1, :] = o_rx[k, 1:2, :]
    for copy in sent:
        copy.wait_send()


def on_device(hidden, norm_gain, head_weight, token_ids, seq_lengths):
    hbm = pl.BlockSpec(memory_space=pl.ANY)
    vmem = pl.BlockSpec(memory_space=pltpu.VMEM)
    smem = pl.BlockSpec(memory_space=pltpu.SMEM)
    f32, bf16, i32 = jnp.float32, jnp.bfloat16, jnp.int32
    dma = pltpu.SemaphoreType.DMA
    lp, ent = pl.pallas_call(
        kernel,
        out_shape=(jax.ShapeDtypeStruct((16, 128), f32), jax.ShapeDtypeStruct((16, 128), f32)),
        in_specs=[hbm, hbm, hbm, hbm, smem],
        out_specs=(vmem, vmem),
        scratch_shapes=[
            pltpu.VMEM((GROUPS, ROWS, 128), bf16),
            pltpu.VMEM((16, ROWS, D), bf16),
            pltpu.VMEM((NCHUNK, D, CHUNK), bf16),
            pltpu.VMEM(head_weight.shape, bf16),
            pltpu.VMEM((ROWS, CHUNK), bf16),
            pltpu.VMEM((GROUPS, 1, 128), f32),
            pltpu.VMEM((GROUPS, 2, 1, 128), i32),
            pltpu.VMEM((16 * ROWS, 128), i32),
            pltpu.VMEM((16 * ROWS, 128), f32),
            pltpu.VMEM((16 * ROWS, 128), f32),
            pltpu.VMEM((16 * ROWS, 128), f32),
            pltpu.VMEM((16 * ROWS, 128), f32),
            pltpu.VMEM((TILE, CHUNK), f32),
            pltpu.VMEM((TILE, CHUNK), f32),
            pltpu.VMEM((16, 4, 128), f32),
            pltpu.VMEM((16, 4, 128), f32),
            pltpu.VMEM((2, 128), f32),
            pltpu.VMEM((16, 2, 128), f32),
            dma((8,)), dma((8,)), dma((8,)), dma((8,)), dma((8,)), dma((8,)),
            dma((40,)), dma((40,)), dma((36,)), dma((36,)), dma((5,)),
            dma((16,)), dma((16,)), dma((16,)), dma((16,)),
        ],
        compiler_params=pltpu.CompilerParams(
            collective_id=0, has_side_effects=True, vmem_limit_bytes=56 * 2**20),
        name="score",
    )(hidden, head_weight, norm_gain.reshape(1, 128), token_ids.reshape(2, GROUPS, 1, 128), seq_lengths)
    return lp.reshape(2048), ent.reshape(2048)


def solution(mesh):
    in_specs = (P("vocab", "width"), P("width"), P("width", "vocab"), P("width"), P())
    out_specs = (P("width"), P("width"))
    return jax.shard_map(
        on_device, mesh=mesh, in_specs=in_specs, out_specs=out_specs, check_vma=False
    )
```

```python
import jax
import jax.numpy as jnp
from jax import lax
from jax.experimental import pallas as pl
from jax.experimental.pallas import tpu as pltpu
from jax.sharding import PartitionSpec as P

D = 1024
SEQ_LEN = 2048
SEQS = 8
SIDE = 4
GROUPS = 8
ROWS = 128
HALF = 64
CHUNK = 512
NCHUNK = 4
TILE = 256
NEG = -1e30
MESH = pl.DeviceIdType.MESH
UNITS = [(0, 0, 0), (1, 0, 0), (0, 0, 1), (1, 1, 0),
         (0, 0, 3), (1, 3, 0), (0, 1, 0), (1, 0, 1),
         (0, 3, 0), (1, 0, 3), (0, 0, 2), (1, 2, 0),
         (0, 1, 1), (1, 1, 1), (0, 3, 1), (1, 1, 3),
         (0, 1, 3), (1, 3, 1), (0, 3, 3), (1, 3, 3),
         (0, 2, 0), (1, 0, 2), (0, 1, 2), (1, 2, 1),
         (0, 3, 2), (1, 2, 3), (0, 2, 1), (1, 1, 2),
         (0, 2, 3), (1, 3, 2), (0, 2, 2), (1, 2, 2)]
PLACE = {d: i for i, d in enumerate(UNITS)}
NTILE = 8
STEPS = [(0, 0), (1, 0), (2, 0), (0, 1), (1, 1), (2, 1), (3, 0), (3, 1),
         (0, 2), (1, 2), (2, 2), (3, 2), (4, 0), (4, 1), (4, 2), (4, 3),
         (3, 3), (2, 3), (5, 0), (5, 1), (5, 2), (5, 3), (6, 0), (6, 1),
         (6, 2), (6, 3), (7, 0), (7, 1), (7, 2), (7, 3), (1, 3), (0, 3)]
PART = 256
NPART = 8


def kernel(hid, head, gain, ids, lens, out,
           xin, xn, wb, aux, idl, m, s, u, t, lb0, lb1, st_tx, st_rx, o_tx, lens_v, gain_v, ids_v, aux_tx,
           as_, ar, gs, gr, is_, xs, xr, ws, wr, wl, ss_, sr, os_, or_, ls_):
    v = lax.axis_index("vocab")
    w = lax.axis_index("width")
    z, x = v // SIDE, v % SIDE
    y, c = w // 2, w % 2
    columns = head.shape[0]

    def at(dz, dx):
        return (lax.rem(z + dz + SIDE, SIDE) * SIDE + lax.rem(x + dx + SIDE, SIDE), w)

    def up(dy, other=0):
        return (v, lax.rem(y + dy + SIDE, SIDE) * 2 + (1 - c if other else c))

    def group(d):
        return lax.rem(w + d, GROUPS)

    def remote(src, dst, send, recv, dev):
        return pltpu.make_async_remote_copy(src_ref=src, dst_ref=dst, send_sem=send, recv_sem=recv,
                                            device_id=dev, device_id_type=MESH)

    barrier = pltpu.get_barrier_semaphore()
    peers = [(v, group(d)) for d in range(1, GROUPS)] + [at(0, 1), at(0, -1), at(1, 0), at(-1, 0)]
    for dev in peers:
        pl.semaphore_signal(barrier, inc=1, device_id=dev, device_id_type=MESH)
    own_gain = pltpu.make_async_copy(gain, gain_v, gs.at[0])
    own_ids = pltpu.make_async_copy(ids, ids_v, is_.at[0])
    lens_copy = pltpu.make_async_copy(lens, lens_v, ls_.at[0])
    for copy in (own_gain, own_ids, lens_copy):
        copy.start()
    for copy in (own_gain, own_ids, lens_copy):
        copy.wait()
    for g in range(GROUPS):
        for k in (0, 1):
            aux_tx[g, k:k + 1, :] = ids_v[k, g].astype(jnp.float32)
        aux_tx[g, 2:3, :] = gain_v[...]
    pl.semaphore_wait(barrier, len(peers))

    sent = []

    def go(copy):
        copy.start()
        sent.append(copy)

    a_copies, g_copies = {0: [], 1: []}, []
    own = []
    for h in (0, 1):
        for d in range(GROUPS):
            g = group(d)
            rows = pl.ds(pl.multiple_of(g * ROWS + h * HALF, HALF), HALF)
            place = xin.at[w, pl.ds(h * HALF, HALF), :]
            if d == 0:
                own.append(pltpu.make_async_copy(hid.at[rows, :], place, as_.at[h, 0]))
            else:
                a_copies[h].append(remote(hid.at[rows, :], place, as_.at[h, d], ar.at[h, d], (v, g)))
    for d in range(1, GROUPS):
        g = group(d)
        g_copies.append(remote(aux_tx.at[g], aux.at[w], gs.at[d], gr.at[d], (v, g)))
    def wcols(dy):
        src = lax.rem(y - dy + SIDE, SIDE) * 2 + c
        return pl.ds(pl.multiple_of(src * 128, 128), 128)

    W = {}
    wlocal = {}
    for j in range(NPART):
        n = min(PART, columns - j * PART)
        mine = head.at[pl.ds(j * PART, n), :]
        mid = PART // 2
        row0 = j % 2 * PART

        def wv(dy, lo=0, hi=n):
            return wb.at[j // 2, pl.ds(row0 + lo, hi - lo), wcols(dy)]

        def wcopy(k, src, dst, dev):
            W[j, k] = remote(src, dst, ws.at[j * 9 + k], wr.at[j * 9 + k], dev)

        wcopy(0, mine, wv(0), up(1))
        wcopy(1, mine, wv(0), up(-1))
        wcopy(2, mine, wv(0), up(0, 1))
        wcopy(3, wv(1, 0, mid), wv(1, 0, mid), up(1))
        wcopy(4, wv(1), wv(1), up(0, 1))
        wcopy(5, wv(3, mid), wv(3, mid), up(-1))
        wcopy(6, wv(3), wv(3), up(0, 1))
        wcopy(7, wv(2, 0, mid), wv(2, 0, mid), up(0, 1))
        wcopy(8, wv(2, mid), wv(2, mid), up(0, 1))
        wlocal[j] = pltpu.make_async_copy(mine, wv(0), wl.at[j])

    def w_own(j):
        for k in (0, 1, 2):
            go(W[j, k])
        wlocal[j].start()

    def w_forward(j):
        W[j, 0].wait_recv()
        go(W[j, 3])
        W[j, 1].wait_recv()
        go(W[j, 5])
        go(W[j, 4])
        go(W[j, 6])

    def w_across(j):
        W[j, 3].wait_recv()
        go(W[j, 7])
        W[j, 5].wait_recv()
        go(W[j, 8])

    def w_done(chunk):
        for j in (2 * chunk, 2 * chunk + 1):
            wlocal[j].wait()
            for k in (2, 4, 6, 7, 8):
                W[j, k].wait_recv()

    X = {}

    def turn(h, a, b):
        return (b, a) if h == 0 else (a, b)

    def xcopy(name, h, d, lo, n, step):
        to = ((d[0] + step[0]) % SIDE, (d[1] + step[1]) % SIDE)
        k = len(X)
        X[name] = remote(xn.at[PLACE[h, *d], pl.ds(lo, n), :], xn.at[PLACE[h, *to], pl.ds(lo, n), :],
                         xs.at[k], xr.at[k], at(*step))

    for h in (0, 1):
        for sgn, near in ((1, 1), (-1, 3)):
            q = 0 if sgn == 1 else 32
            xcopy((h, "first", near), h, (0, 0), 0, 64, turn(h, sgn, 0))
            xcopy((h, "first", 2, near), h, turn(h, near, 0), q, 32, turn(h, sgn, 0))
            for far in range(SIDE):
                xcopy((h, "second", far, near), h, turn(h, far, 0), 0, 64, turn(h, 0, sgn))
                xcopy((h, "last", far, near), h, turn(h, far, near), q, 32, turn(h, 0, sgn))

    def x_own(h):
        for near in (1, 3):
            go(X[h, "first", near])

    def x_own_across():
        for h in (0, 1):
            for near in (1, 3):
                go(X[h, "second", 0, near])

    def x_round1():
        for h in (0, 1):
            for near in (1, 3):
                X[h, "first", near].wait_recv()
                go(X[h, "first", 2, near])

    def x_near(near):
        for h in (0, 1):
            for side in (1, 3):
                go(X[h, "second", near, side])

    def x_pace():
        for h in (0, 1):
            for near in (1, 3):
                X[h, "second", 0, near].wait_recv()

    def x_round2():
        for h in (0, 1):
            for near in (1, 3):
                go(X[h, "last", 0, near])

    def x_round3_wait():
        for h in (0, 1):
            for near in (1, 3):
                X[h, "first", 2, near].wait_recv()

    def x_round3():
        for h in (0, 1):
            for side in (1, 3):
                go(X[h, "second", 2, side])

    def x_round4(far):
        for h in (0, 1):
            for near in (1, 3):
                X[h, "second", far, near].wait_recv()
                go(X[h, "last", far, near])

    def x_round5():
        for h in (0, 1):
            for near in (1, 3):
                X[h, "second", 2, near].wait_recv()
                go(X[h, "last", 2, near])

    def x_last(far):
        for h in (0, 1):
            for near in (1, 3):
                X[h, "last", far, near].wait_recv()

    far_first = (3, 4, 2, 5, 1, 6, 0)
    for k in far_first:
        go(a_copies[0][k])
    w_own(0)
    for copy in g_copies:
        go(copy)
    for k in far_first:
        go(a_copies[1][k])
    w_own(1)
    for copy in own:
        copy.start()
    aux[w] = aux_tx[w]

    m[...] = jnp.full(m.shape, NEG, jnp.float32)
    for ref in (s, u, t):
        ref[...] = jnp.zeros(ref.shape, jnp.float32)

    w_forward(0)
    w_own(2)

    for h in (0, 1):
        own[h].wait()
        for copy in a_copies[h]:
            copy.wait_recv()
        if h == 0:
            for copy in g_copies:
                copy.wait_recv()
        for r in range(0, HALF, 32):
            wide = [xin[k, h * HALF + r:h * HALF + r + 32, :].astype(jnp.float32) for k in range(GROUPS)]
            squares = wide[0] * wide[0]
            for k in range(1, GROUPS):
                squares = squares + wide[k] * wide[k]
            scale = lax.rsqrt(jnp.sum(squares, axis=1, keepdims=True) / D + 1e-06)
            for k in range(GROUPS):
                xn[h, r:r + 32, k * 128:(k + 1) * 128] = (wide[k] * scale * aux[k, 2:3, :]).astype(jnp.bfloat16)
        x_own(h)
        if h == 0:
            w_own(3)

    w_across(0)
    x_own_across()

    which = lax.broadcasted_iota(jnp.int32, (1, SEQS), 1) == v // 2
    limit = jnp.sum(jnp.where(which, lens_v[...], 0), axis=1, keepdims=True)

    lane = lax.broadcasted_iota(jnp.int32, (ROWS, 128), 1)
    base = v * columns
    for dz in range(SIDE):
        for dx in range(SIDE):
            block = lax.rem(z - dz + SIDE, SIDE) * SIDE + lax.rem(x - dx + SIDE, SIDE)
            row = aux[block // 2, pl.ds(block % 2, 1), :].astype(jnp.int32)
            row = jnp.where(row - base < columns, row - base, -1)
            wide = jnp.broadcast_to(row, (ROWS, 128)).T - lane
            for h in (0, 1):
                idl[PLACE[h, dz, dx]] = wide[h * HALF:(h + 1) * HALF, :]

    w_forward(1)
    w_own(4)
    x_round1()
    x_near(1)
    w_across(1)
    w_forward(2)
    w_own(5)
    w_done(0)

    def pick(values, i):
        out = jnp.int32(values[0])
        for k in range(1, len(values)):
            if values[k] != values[k - 1]:
                out = jnp.where(i >= k, jnp.int32(values[k]), out)
        return out

    def tile_of(i):
        return pick([p for p, _ in STEPS], i), pick([j for _, j in STEPS], i)

    def dot(i, buf):
        p, j = tile_of(i)
        lhs = xn[pl.ds(p * 4, 4)].reshape(TILE, D)
        buf[...] = lax.dot_general(lhs, wb[j], (((1,), (1,)), ((), ())), preferred_element_type=jnp.float32)

    group_rows = 16
    parts = CHUNK // 128
    lane_g = lax.broadcasted_iota(jnp.int32, (group_rows, 128), 1)

    def stats(i, buf):
        p, j = tile_of(i)
        col0 = j * CHUNK
        edge = lane_g < columns - (parts - 1) * 128 - col0
        for g in range(TILE // group_rows):
            at_rows = (p * 4 + g * group_rows // HALF, pl.ds(g * group_rows % HALF, group_rows))
            ls = [buf[g * group_rows:(g + 1) * group_rows, k * 128:(k + 1) * 128] for k in range(parts)]
            ls[-1] = jnp.where(edge, ls[-1], NEG)
            m_old = m[at_rows]
            top = jnp.maximum(jnp.maximum(ls[0], ls[1]), jnp.maximum(ls[2], ls[3]))
            m_new = jnp.maximum(m_old, top)
            fade = jnp.exp(m_old - m_new)
            s_new = s[at_rows] * fade
            u_new = u[at_rows] * fade
            t_new = t[at_rows]
            here = idl[at_rows]
            for k in range(parts):
                e = jnp.exp(ls[k] - m_new)
                s_new = s_new + e
                u_new = u_new + e * ls[k]
                t_new = jnp.where(here == col0 + k * 128, ls[k], t_new)
            m[at_rows] = m_new
            s[at_rows] = s_new
            u[at_rows] = u_new
            t[at_rows] = t_new

    def finish(q):
        def rows_of(ref):
            return ref[pl.ds(q * 2, 2)].reshape(ROWS, 128).T

        mt = rows_of(m)
        peak = jnp.max(mt, axis=0, keepdims=True)
        scale = jnp.exp(mt - peak)
        st_tx[q, 0:1, :] = peak
        st_tx[q, 1:2, :] = jnp.sum(rows_of(s) * scale, axis=0, keepdims=True)
        st_tx[q, 2:3, :] = jnp.sum(rows_of(u) * scale, axis=0, keepdims=True)
        st_tx[q, 3:4, :] = jnp.sum(rows_of(t), axis=0, keepdims=True)

    S = {}
    for k, (h, dz, dx) in enumerate(UNITS):
        if k >= 2 and not (k % 2 == 1 and UNITS[k - 1][1:] == (dz, dx)):
            S[k] = remote(st_tx.at[k // 2], st_rx.at[k], ss_.at[k], sr.at[k], at(-dz, -dx))

    def send_stats(tile):
        for k in range(tile * 4, tile * 4 + 4):
            if k in S:
                go(S[k])

    def finish_tile(tile):
        finish(tile * 2)
        finish(tile * 2 + 1)
        send_stats(tile)

    def acts_0():
        w_forward(3)
        w_own(6)
        x_near(3)
        x_pace()
        w_across(2)
        x_round2()
        w_forward(4)
        w_own(7)
        x_round3_wait()
        x_round3()

    def acts_1():
        w_across(3)
        w_forward(5)
        w_done(1)

    def acts_2():
        w_across(4)
        x_round4(1)
        w_forward(6)

    def acts_3():
        w_across(5)
        w_forward(7)
        w_done(2)

    def acts_4():
        x_round4(3)

    def acts_5():
        w_across(6)

    def acts_6():
        w_across(7)
        x_round5()

    def acts_7():
        w_done(3)

    def acts_8():
        x_last(0)
        finish_tile(4)

    def acts_9():
        finish_tile(3)
        finish_tile(2)

    def acts_10():
        x_last(1)

    def acts_11():
        finish_tile(5)

    def acts_12():
        x_last(3)
        x_last(2)

    def acts_13():
        finish_tile(6)

    def acts_15():
        finish_tile(7)

    ACTS = {0: acts_0, 1: acts_1, 2: acts_2, 3: acts_3, 4: acts_4, 5: acts_5, 6: acts_6, 7: acts_7, 8: acts_8,
            9: acts_9, 10: acts_10, 11: acts_11, 12: acts_12, 13: acts_13, 15: acts_15}
    total = len(STEPS)
    dot(0, lb0)

    @pl.loop(0, total // 2)
    def _(h):
        i = h * 2
        for k in ACTS:
            pl.when(h == k)(ACTS[k])
        dot(i + 1, lb1)
        stats(i, lb0)
        dot(jnp.minimum(i + 2, total - 1), lb0)
        stats(i + 1, lb1)

    for tile in (1, 0):
        finish_tile(tile)
    for copy in S.values():
        copy.wait_recv()

    first_half = lax.broadcasted_iota(jnp.int32, (4, 128), 1) < HALF

    def stat_of(dz, dx):
        if (dz, dx) == (0, 0):
            return st_tx[0]
        a, b = PLACE[0, dz, dx], PLACE[1, dz, dx]
        if b not in S:
            return st_rx[a]
        return jnp.where(first_half, st_rx[a], st_rx[b])

    stat = [stat_of(dz, dx) for dz in range(SIDE) for dx in range(SIDE)]
    peak = stat[0][0:1, :]
    for a in stat[1:]:
        peak = jnp.maximum(peak, a[0:1, :])
    sum_e = jnp.zeros_like(peak)
    sum_w = jnp.zeros_like(peak)
    target = jnp.zeros_like(peak)
    for a in stat:
        f = jnp.exp(a[0:1, :] - peak)
        sum_e = sum_e + a[1:2, :] * f
        sum_w = sum_w + a[2:3, :] * f
        target = target + a[3:4, :]
    log_total = peak + jnp.log(sum_e)
    position = lax.rem(v, 2) * (SEQ_LEN // 2) + w * ROWS + lax.broadcasted_iota(jnp.int32, (1, 128), 1)
    live = position < limit
    o_tx[0] = jnp.where(live, target - log_total, 0.0)
    o_tx[1] = jnp.where(live, log_total - sum_w / sum_e, 0.0)

    goal = v // 2
    mine = lax.rem(v, 2) * GROUPS + w

    def result(k, place, dev):
        return remote(o_tx, out.at[:, place], os_.at[k], or_.at[place], dev)

    o_own = pltpu.make_async_copy(o_tx, out.at[:, mine], os_.at[16])
    for k in range(16):
        @pl.when(jnp.logical_not(jnp.logical_and(k == v, goal == w)))
        def _():
            result(k, mine, (k, goal)).start()

    @pl.when(goal == w)
    def _():
        o_own.start()

    for copy in sent:
        copy.wait_send()
    for k in range(16):
        @pl.when(jnp.logical_not(jnp.logical_and(2 * w + k // GROUPS == v, k % GROUPS == w)))
        def _():
            result(k, k, (v, w)).wait_recv()

        @pl.when(jnp.logical_not(jnp.logical_and(k == v, goal == w)))
        def _():
            result(k, mine, (k, goal)).wait_send()

    @pl.when(goal == w)
    def _():
        o_own.wait()


def on_device(hidden, norm_gain, head_weight, token_ids, seq_lengths):
    hbm = pl.BlockSpec(memory_space=pl.ANY)
    f32, bf16, i32 = jnp.float32, jnp.bfloat16, jnp.int32
    dma = pltpu.SemaphoreType.DMA
    rows = pltpu.VMEM((32, HALF, 128), f32)
    scores = pl.pallas_call(
        kernel,
        out_shape=jax.ShapeDtypeStruct((2, 16, 1, 128), f32),
        in_specs=[hbm, hbm, hbm, hbm, hbm],
        out_specs=hbm,
        scratch_shapes=[
            pltpu.VMEM((GROUPS, ROWS, 128), bf16),
            pltpu.VMEM((32, HALF, D), bf16),
            pltpu.VMEM((NCHUNK, CHUNK, D), bf16),
            pltpu.VMEM((GROUPS, 3, 128), f32),
            pltpu.VMEM((32, HALF, 128), i32),
            rows, rows, rows, rows,
            pltpu.VMEM((TILE, CHUNK), f32),
            pltpu.VMEM((TILE, CHUNK), f32),
            pltpu.VMEM((16, 4, 128), f32),
            pltpu.VMEM((32, 4, 128), f32),
            pltpu.VMEM((2, 1, 128), f32),
            pltpu.VMEM((1, SEQS), i32),
            pltpu.VMEM((1, 128), f32),
            pltpu.VMEM((2, GROUPS, 1, 128), i32),
            pltpu.VMEM((GROUPS, 3, 128), f32),
            dma((2, 8)), dma((2, 8)), dma((8,)), dma((8,)), dma((1,)),
            dma((40,)), dma((40,)), dma((72,)), dma((72,)), dma((8,)),
            dma((32,)), dma((32,)), dma((17,)), dma((16,)), dma((1,)),
        ],
        compiler_params=pltpu.CompilerParams(
            collective_id=0, has_side_effects=True, vmem_limit_bytes=56 * 2**20),
        name="score",
    )(hidden, head_weight.T, norm_gain.reshape(1, 128), token_ids.reshape(2, GROUPS, 1, 128),
      seq_lengths.reshape(1, SEQS))
    return scores[0].reshape(SEQ_LEN), scores[1].reshape(SEQ_LEN)


def solution(mesh):
    in_specs = (P("vocab", "width"), P("width"), P("width", "vocab"), P("width"), P())
    out_specs = (P("width"), P("width"))
    return jax.shard_map(
        on_device, mesh=mesh, in_specs=in_specs, out_specs=out_specs, check_vma=False
    )
```

```python
import jax
import jax.numpy as jnp
from jax import lax
from jax.experimental import pallas as pl
from jax.experimental.pallas import tpu as pltpu
from jax.sharding import PartitionSpec as P

D = 1024
SEQ_LEN = 2048
SEQS = 8
SIDE = 4
GROUPS = 8
ROWS = 128
HALF = 64
CHUNK = 512
NCHUNK = 4
TILE = 256
NEG = -1e30
MESH = pl.DeviceIdType.MESH
UNITS = [(0, 0, 0), (1, 0, 0), (0, 0, 1), (1, 1, 0),
         (0, 0, 3), (1, 3, 0), (0, 1, 0), (1, 0, 1),
         (0, 3, 0), (1, 0, 3), (0, 0, 2), (1, 2, 0),
         (0, 1, 1), (1, 1, 1), (0, 3, 1), (1, 1, 3),
         (0, 1, 3), (1, 3, 1), (0, 3, 3), (1, 3, 3),
         (0, 2, 0), (1, 0, 2), (0, 1, 2), (1, 2, 1),
         (0, 3, 2), (1, 2, 3), (0, 2, 1), (1, 1, 2),
         (0, 2, 3), (1, 3, 2), (0, 2, 2), (1, 2, 2)]
PLACE = {d: i for i, d in enumerate(UNITS)}
NTILE = 8
STEPS = [(0, 0), (1, 0), (2, 0), (0, 1), (1, 1), (2, 1), (3, 0), (3, 1),
         (0, 2), (1, 2), (2, 2), (3, 2), (4, 0), (4, 1), (4, 2), (4, 3),
         (3, 3), (2, 3), (5, 0), (5, 1), (5, 2), (5, 3), (6, 0), (6, 1),
         (6, 2), (6, 3), (7, 0), (7, 1), (7, 2), (7, 3), (1, 3), (0, 3)]
PART = 256
NPART = 8


def kernel(hid, head, gain, ids, lens, out,
           xin, xn, wb, aux, idl, m, s, u, t, lb0, lb1, st_tx, st_rx, o_tx, lens_v, gain_v, ids_v, aux_tx,
           as_, ar, gs, gr, is_, xs, xr, ws, wr, wl, ss_, sr, os_, or_, ls_):
    v = lax.axis_index("vocab")
    w = lax.axis_index("width")
    z, x = v // SIDE, v % SIDE
    y, c = w // 2, w % 2
    columns = head.shape[0]

    def at(dz, dx):
        return (lax.rem(z + dz + SIDE, SIDE) * SIDE + lax.rem(x + dx + SIDE, SIDE), w)

    def up(dy, other=0):
        return (v, lax.rem(y + dy + SIDE, SIDE) * 2 + (1 - c if other else c))

    def group(d):
        return lax.rem(w + d, GROUPS)

    def remote(src, dst, send, recv, dev):
        return pltpu.make_async_remote_copy(src_ref=src, dst_ref=dst, send_sem=send, recv_sem=recv,
                                            device_id=dev, device_id_type=MESH)

    barrier = pltpu.get_barrier_semaphore()
    peers = [(v, group(d)) for d in range(1, GROUPS)] + [at(0, 1), at(0, -1), at(1, 0), at(-1, 0)]
    for dev in peers:
        pl.semaphore_signal(barrier, inc=1, device_id=dev, device_id_type=MESH)
    own_gain = pltpu.make_async_copy(gain, gain_v, gs.at[0])
    own_ids = pltpu.make_async_copy(ids, ids_v, is_.at[0])
    lens_copy = pltpu.make_async_copy(lens, lens_v, ls_.at[0])
    for copy in (own_gain, own_ids, lens_copy):
        copy.start()
    for copy in (own_gain, own_ids, lens_copy):
        copy.wait()
    for g in range(GROUPS):
        for k in (0, 1):
            aux_tx[g, k:k + 1, :] = ids_v[k, g].astype(jnp.float32)
        aux_tx[g, 2:3, :] = gain_v[...]
    pl.semaphore_wait(barrier, len(peers))

    sent = []

    def go(copy):
        copy.start()
        sent.append(copy)

    a_copies, g_copies = {0: [], 1: []}, []
    own = []
    for h in (0, 1):
        for d in range(GROUPS):
            g = group(d)
            rows = pl.ds(pl.multiple_of(g * ROWS + h * HALF, HALF), HALF)
            place = xin.at[w, pl.ds(h * HALF, HALF), :]
            if d == 0:
                own.append(pltpu.make_async_copy(hid.at[rows, :], place, as_.at[h, 0]))
            else:
                a_copies[h].append(remote(hid.at[rows, :], place, as_.at[h, d], ar.at[h, d], (v, g)))
    for d in range(1, GROUPS):
        g = group(d)
        g_copies.append(remote(aux_tx.at[g], aux.at[w], gs.at[d], gr.at[d], (v, g)))
    def wcols(dy):
        src = lax.rem(y - dy + SIDE, SIDE) * 2 + c
        return pl.ds(pl.multiple_of(src * 128, 128), 128)

    W = {}
    wlocal = {}
    for j in range(NPART):
        n = min(PART, columns - j * PART)
        mine = head.at[pl.ds(j * PART, n), :]
        mid = PART // 2
        row0 = j % 2 * PART

        def wv(dy, lo=0, hi=n):
            return wb.at[j // 2, pl.ds(row0 + lo, hi - lo), wcols(dy)]

        def wcopy(k, src, dst, dev):
            W[j, k] = remote(src, dst, ws.at[j * 9 + k], wr.at[j * 9 + k], dev)

        wcopy(0, mine, wv(0), up(1))
        wcopy(1, mine, wv(0), up(-1))
        wcopy(2, mine, wv(0), up(0, 1))
        wcopy(3, wv(1, 0, mid), wv(1, 0, mid), up(1))
        wcopy(4, wv(1), wv(1), up(0, 1))
        wcopy(5, wv(3, mid), wv(3, mid), up(-1))
        wcopy(6, wv(3), wv(3), up(0, 1))
        wcopy(7, wv(2, 0, mid), wv(2, 0, mid), up(0, 1))
        wcopy(8, wv(2, mid), wv(2, mid), up(0, 1))
        wlocal[j] = pltpu.make_async_copy(mine, wv(0), wl.at[j])

    def w_own(j):
        for k in (0, 1, 2):
            go(W[j, k])
        wlocal[j].start()

    def w_forward(j):
        W[j, 0].wait_recv()
        go(W[j, 3])
        W[j, 1].wait_recv()
        go(W[j, 5])
        go(W[j, 4])
        go(W[j, 6])

    def w_across(j):
        W[j, 3].wait_recv()
        go(W[j, 7])
        W[j, 5].wait_recv()
        go(W[j, 8])

    def w_done(chunk):
        for j in (2 * chunk, 2 * chunk + 1):
            wlocal[j].wait()
            for k in (2, 4, 6, 7, 8):
                W[j, k].wait_recv()

    X = {}

    def turn(h, a, b):
        return (b, a) if h == 0 else (a, b)

    def xcopy(name, h, d, lo, n, step):
        to = ((d[0] + step[0]) % SIDE, (d[1] + step[1]) % SIDE)
        k = len(X)
        X[name] = remote(xn.at[PLACE[h, *d], pl.ds(lo, n), :], xn.at[PLACE[h, *to], pl.ds(lo, n), :],
                         xs.at[k], xr.at[k], at(*step))

    for h in (0, 1):
        for sgn, near in ((1, 1), (-1, 3)):
            q = 0 if sgn == 1 else 32
            xcopy((h, "first", near), h, (0, 0), 0, 64, turn(h, sgn, 0))
            xcopy((h, "first", 2, near), h, turn(h, near, 0), q, 32, turn(h, sgn, 0))
            for far in range(SIDE):
                xcopy((h, "second", far, near), h, turn(h, far, 0), 0, 64, turn(h, 0, sgn))
                xcopy((h, "last", far, near), h, turn(h, far, near), q, 32, turn(h, 0, sgn))

    def x_own(h):
        for near in (1, 3):
            go(X[h, "first", near])

    def x_own_across():
        for h in (0, 1):
            for near in (1, 3):
                go(X[h, "second", 0, near])

    def x_round1():
        for h in (0, 1):
            for near in (1, 3):
                X[h, "first", near].wait_recv()
                go(X[h, "first", 2, near])

    def x_near(near):
        for h in (0, 1):
            for side in (1, 3):
                go(X[h, "second", near, side])

    def x_pace():
        for h in (0, 1):
            for near in (1, 3):
                X[h, "second", 0, near].wait_recv()

    def x_round2():
        for h in (0, 1):
            for near in (1, 3):
                go(X[h, "last", 0, near])

    def x_round3_wait():
        for h in (0, 1):
            for near in (1, 3):
                X[h, "first", 2, near].wait_recv()

    def x_round3():
        for h in (0, 1):
            for side in (1, 3):
                go(X[h, "second", 2, side])

    def x_round4(far):
        for h in (0, 1):
            for near in (1, 3):
                X[h, "second", far, near].wait_recv()
                go(X[h, "last", far, near])

    def x_round5():
        for h in (0, 1):
            for near in (1, 3):
                X[h, "second", 2, near].wait_recv()
                go(X[h, "last", 2, near])

    def x_last(far):
        for h in (0, 1):
            for near in (1, 3):
                X[h, "last", far, near].wait_recv()

    far_first = (3, 4, 2, 5, 1, 6, 0)
    for copy in g_copies:
        go(copy)
    for k in far_first:
        go(a_copies[0][k])
    w_own(0)
    for k in far_first:
        go(a_copies[1][k])
    w_own(1)
    for copy in own:
        copy.start()
    aux[w] = aux_tx[w]

    m[...] = jnp.full(m.shape, NEG, jnp.float32)
    for ref in (s, u, t):
        ref[...] = jnp.zeros(ref.shape, jnp.float32)

    w_forward(0)
    w_own(2)

    for h in (0, 1):
        own[h].wait()
        for copy in a_copies[h]:
            copy.wait_recv()
        if h == 0:
            for copy in g_copies:
                copy.wait_recv()
        for r in range(0, HALF, 32):
            wide = [xin[k, h * HALF + r:h * HALF + r + 32, :].astype(jnp.float32) for k in range(GROUPS)]
            squares = wide[0] * wide[0]
            for k in range(1, GROUPS):
                squares = squares + wide[k] * wide[k]
            scale = lax.rsqrt(jnp.sum(squares, axis=1, keepdims=True) / D + 1e-06)
            for k in range(GROUPS):
                xn[h, r:r + 32, k * 128:(k + 1) * 128] = (wide[k] * scale * aux[k, 2:3, :]).astype(jnp.bfloat16)
        x_own(h)
        if h == 0:
            w_own(3)

    w_across(0)
    x_own_across()

    which = lax.broadcasted_iota(jnp.int32, (1, SEQS), 1) == v // 2
    limit = jnp.sum(jnp.where(which, lens_v[...], 0), axis=1, keepdims=True)

    lane = lax.broadcasted_iota(jnp.int32, (ROWS, 128), 1)
    base = v * columns
    for dz in range(SIDE):
        for dx in range(SIDE):
            block = lax.rem(z - dz + SIDE, SIDE) * SIDE + lax.rem(x - dx + SIDE, SIDE)
            row = aux[block // 2, pl.ds(block % 2, 1), :].astype(jnp.int32)
            row = jnp.where(row - base < columns, row - base, -1)
            wide = jnp.broadcast_to(row, (ROWS, 128)).T - lane
            for h in (0, 1):
                idl[PLACE[h, dz, dx]] = wide[h * HALF:(h + 1) * HALF, :]

    w_forward(1)
    w_own(4)
    w_forward(2)
    x_round1()
    x_near(1)
    w_forward(3)
    w_own(5)
    w_across(1)
    w_own(6)
    w_done(0)

    def pick(values, i):
        out = jnp.int32(values[0])
        for k in range(1, len(values)):
            if values[k] != values[k - 1]:
                out = jnp.where(i >= k, jnp.int32(values[k]), out)
        return out

    def tile_of(i):
        return pick([p for p, _ in STEPS], i), pick([j for _, j in STEPS], i)

    def dot(i, buf):
        p, j = tile_of(i)
        lhs = xn[pl.ds(p * 4, 4)].reshape(TILE, D)
        buf[...] = lax.dot_general(lhs, wb[j], (((1,), (1,)), ((), ())), preferred_element_type=jnp.float32)

    group_rows = 16
    parts = CHUNK // 128
    lane_g = lax.broadcasted_iota(jnp.int32, (group_rows, 128), 1)

    def stats(i, buf):
        p, j = tile_of(i)
        col0 = j * CHUNK
        edge = lane_g < columns - (parts - 1) * 128 - col0
        for g in range(TILE // group_rows):
            at_rows = (p * 4 + g * group_rows // HALF, pl.ds(g * group_rows % HALF, group_rows))
            ls = [buf[g * group_rows:(g + 1) * group_rows, k * 128:(k + 1) * 128] for k in range(parts)]
            ls[-1] = jnp.where(edge, ls[-1], NEG)
            m_old = m[at_rows]
            top = jnp.maximum(jnp.maximum(ls[0], ls[1]), jnp.maximum(ls[2], ls[3]))
            m_new = jnp.maximum(m_old, top)
            fade = jnp.exp(m_old - m_new)
            s_new = s[at_rows] * fade
            u_new = u[at_rows] * fade
            t_new = t[at_rows]
            here = idl[at_rows]
            for k in range(parts):
                e = jnp.exp(ls[k] - m_new)
                s_new = s_new + e
                u_new = u_new + e * ls[k]
                t_new = jnp.where(here == col0 + k * 128, ls[k], t_new)
            m[at_rows] = m_new
            s[at_rows] = s_new
            u[at_rows] = u_new
            t[at_rows] = t_new

    def finish(q, place=None):
        place = q if place is None else place

        def rows_of(ref):
            return ref[pl.ds(q * 2, 2)].reshape(ROWS, 128).T

        mt = rows_of(m)
        peak = jnp.max(mt, axis=0, keepdims=True)
        scale = jnp.exp(mt - peak)
        st_tx[place, 0:1, :] = peak
        st_tx[place, 1:2, :] = jnp.sum(rows_of(s) * scale, axis=0, keepdims=True)
        st_tx[place, 2:3, :] = jnp.sum(rows_of(u) * scale, axis=0, keepdims=True)
        st_tx[place, 3:4, :] = jnp.sum(rows_of(t), axis=0, keepdims=True)

    S = {}
    for k, (h, dz, dx) in enumerate(UNITS):
        if k >= 2 and not (k % 2 == 1 and UNITS[k - 1][1:] == (dz, dx)):
            S[k] = remote(st_tx.at[k // 2], st_rx.at[k], ss_.at[k], sr.at[k], at(-dz, -dx))

    def send_stats(tile):
        for k in range(tile * 4, tile * 4 + 4):
            if k in S:
                go(S[k])

    def finish_tile(tile):
        finish(tile * 2)
        finish(tile * 2 + 1)
        send_stats(tile)

    def acts_0():
        w_forward(4)
        w_own(7)
        w_across(2)
        x_near(3)
        w_across(3)
        x_pace()
        x_round2()
        x_round3_wait()
        x_round3()

    def acts_1():
        w_forward(5)
        w_forward(6)
        w_across(4)
        w_done(1)

    def acts_2():
        w_across(5)
        w_forward(7)
        x_round4(1)

    def acts_3():
        w_across(6)
        w_done(2)

    def acts_4():
        w_across(7)
        x_round4(3)

    def acts_6():
        x_round5()

    def acts_7():
        w_done(3)

    def acts_8():
        x_last(0)

    def acts_9():
        send_stats(4)

    def acts_10():
        send_stats(3)
        x_last(1)

    def acts_11():
        send_stats(2)

    def acts_12():
        send_stats(5)
        x_last(3)
        x_last(2)

    def acts_14():
        send_stats(6)

    EARLY = {0: acts_0, 1: acts_1, 2: acts_2, 3: acts_3, 4: acts_4, 6: acts_6, 7: acts_7}
    LATE = {8: acts_8, 9: acts_9, 10: acts_10, 11: acts_11, 12: acts_12, 14: acts_14}
    READY = [4, 3, 2, 5, 8, 6, 8, 7]
    total = len(STEPS)
    dot(0, lb0)

    def block(h):
        i = h * 2
        dot(i + 1, lb1)
        stats(i, lb0)
        dot(jnp.minimum(i + 2, total - 1), lb0)
        stats(i + 1, lb1)

    @pl.loop(0, 8)
    def _(h):
        for k in EARLY:
            pl.when(h == k)(EARLY[k])
        block(h)

    @pl.loop(8, total // 2)
    def _(h):
        for k in LATE:
            pl.when(h == k)(LATE[k])
        place = pick(READY, h - 8) * 2
        source = jnp.minimum(place, 14)
        finish(source, place)
        finish(source + 1, place + 1)
        block(h)

    send_stats(7)
    for tile in (1, 0):
        finish_tile(tile)
    for copy in S.values():
        copy.wait_recv()

    first_half = lax.broadcasted_iota(jnp.int32, (4, 128), 1) < HALF

    def stat_of(dz, dx):
        if (dz, dx) == (0, 0):
            return st_tx[0]
        a, b = PLACE[0, dz, dx], PLACE[1, dz, dx]
        if b not in S:
            return st_rx[a]
        return jnp.where(first_half, st_rx[a], st_rx[b])

    stat = [stat_of(dz, dx) for dz in range(SIDE) for dx in range(SIDE)]
    peak = stat[0][0:1, :]
    for a in stat[1:]:
        peak = jnp.maximum(peak, a[0:1, :])
    sum_e = jnp.zeros_like(peak)
    sum_w = jnp.zeros_like(peak)
    target = jnp.zeros_like(peak)
    for a in stat:
        f = jnp.exp(a[0:1, :] - peak)
        sum_e = sum_e + a[1:2, :] * f
        sum_w = sum_w + a[2:3, :] * f
        target = target + a[3:4, :]
    log_total = peak + jnp.log(sum_e)
    position = lax.rem(v, 2) * (SEQ_LEN // 2) + w * ROWS + lax.broadcasted_iota(jnp.int32, (1, 128), 1)
    live = position < limit
    o_tx[0] = jnp.where(live, target - log_total, 0.0)
    o_tx[1] = jnp.where(live, log_total - sum_w / sum_e, 0.0)

    goal = v // 2
    mine = lax.rem(v, 2) * GROUPS + w

    def result(k, place, dev):
        return remote(o_tx, out.at[:, place], os_.at[k], or_.at[place], dev)

    o_own = pltpu.make_async_copy(o_tx, out.at[:, mine], os_.at[16])
    for k in range(16):
        @pl.when(jnp.logical_not(jnp.logical_and(k == v, goal == w)))
        def _():
            result(k, mine, (k, goal)).start()

    @pl.when(goal == w)
    def _():
        o_own.start()

    for copy in sent:
        copy.wait_send()
    for k in range(16):
        @pl.when(jnp.logical_not(jnp.logical_and(2 * w + k // GROUPS == v, k % GROUPS == w)))
        def _():
            result(k, k, (v, w)).wait_recv()

        @pl.when(jnp.logical_not(jnp.logical_and(k == v, goal == w)))
        def _():
            result(k, mine, (k, goal)).wait_send()

    @pl.when(goal == w)
    def _():
        o_own.wait()


def on_device(hidden, norm_gain, head_weight, token_ids, seq_lengths):
    hbm = pl.BlockSpec(memory_space=pl.ANY)
    f32, bf16, i32 = jnp.float32, jnp.bfloat16, jnp.int32
    dma = pltpu.SemaphoreType.DMA
    rows = pltpu.VMEM((32, HALF, 128), f32)
    scores = pl.pallas_call(
        kernel,
        out_shape=jax.ShapeDtypeStruct((2, 16, 1, 128), f32),
        in_specs=[hbm, hbm, hbm, hbm, hbm],
        out_specs=hbm,
        scratch_shapes=[
            pltpu.VMEM((GROUPS, ROWS, 128), bf16),
            pltpu.VMEM((32, HALF, D), bf16),
            pltpu.VMEM((NCHUNK, CHUNK, D), bf16),
            pltpu.VMEM((GROUPS, 3, 128), f32),
            pltpu.VMEM((32, HALF, 128), i32),
            rows, rows, rows, rows,
            pltpu.VMEM((TILE, CHUNK), f32),
            pltpu.VMEM((TILE, CHUNK), f32),
            pltpu.VMEM((18, 4, 128), f32),
            pltpu.VMEM((32, 4, 128), f32),
            pltpu.VMEM((2, 1, 128), f32),
            pltpu.VMEM((1, SEQS), i32),
            pltpu.VMEM((1, 128), f32),
            pltpu.VMEM((2, GROUPS, 1, 128), i32),
            pltpu.VMEM((GROUPS, 3, 128), f32),
            dma((2, 8)), dma((2, 8)), dma((8,)), dma((8,)), dma((1,)),
            dma((40,)), dma((40,)), dma((72,)), dma((72,)), dma((8,)),
            dma((32,)), dma((32,)), dma((17,)), dma((16,)), dma((1,)),
        ],
        compiler_params=pltpu.CompilerParams(
            collective_id=0, has_side_effects=True, vmem_limit_bytes=56 * 2**20),
        name="score",
    )(hidden, head_weight.T, norm_gain.reshape(1, 128), token_ids.reshape(2, GROUPS, 1, 128),
      seq_lengths.reshape(1, SEQS))
    return scores[0].reshape(SEQ_LEN), scores[1].reshape(SEQ_LEN)


def solution(mesh):
    in_specs = (P("vocab", "width"), P("width"), P("width", "vocab"), P("width"), P())
    out_specs = (P("width"), P("width"))
    return jax.shard_map(
        on_device, mesh=mesh, in_specs=in_specs, out_specs=out_specs, check_vma=False
    )
```

```python
import jax
import jax.numpy as jnp
from jax import lax
from jax.experimental import pallas as pl
from jax.experimental.pallas import tpu as pltpu
from jax.sharding import PartitionSpec as P

D = 1024
SEQ_LEN = 2048
SEQS = 8
SIDE = 4
GROUPS = 8
ROWS = 128
HALF = 64
CHUNK = 512
NCHUNK = 4
TILE = 256
NEG = -1e30
MESH = pl.DeviceIdType.MESH
UNITS = [(0, 0, 0), (1, 0, 0), (0, 0, 1), (1, 1, 0),
         (0, 0, 3), (1, 3, 0), (0, 1, 0), (1, 0, 1),
         (0, 3, 0), (1, 0, 3), (0, 0, 2), (1, 2, 0),
         (0, 1, 1), (1, 1, 1), (0, 3, 1), (1, 1, 3),
         (0, 1, 3), (1, 3, 1), (0, 3, 3), (1, 3, 3),
         (0, 2, 0), (1, 0, 2), (0, 1, 2), (1, 2, 1),
         (0, 3, 2), (1, 2, 3), (0, 2, 1), (1, 1, 2),
         (0, 2, 3), (1, 3, 2), (0, 2, 2), (1, 2, 2)]
PLACE = {d: i for i, d in enumerate(UNITS)}
NTILE = 8
STEPS = [(0, 0), (1, 0), (2, 0), (0, 1), (1, 1), (2, 1), (3, 0), (3, 1),
         (0, 2), (1, 2), (2, 2), (3, 2), (4, 0), (4, 1), (4, 2), (4, 3),
         (5, 0), (5, 1), (5, 2), (5, 3), (6, 0), (6, 1), (6, 2), (6, 3),
         (7, 0), (7, 1), (7, 2), (7, 3), (3, 3), (2, 3), (1, 3), (0, 3)]
PART = 256
NPART = 8


def kernel(hid, head, gain, ids, lens, out,
           xin, xn, wb, aux, idl, m, s, u, t, lb0, lb1, st_tx, st_rx, o_tx, lens_v, gain_v, ids_v, aux_tx,
           as_, ar, gs, gr, is_, xs, xr, ws, wr, wl, ss_, sr, os_, or_, ls_):
    v = lax.axis_index("vocab")
    w = lax.axis_index("width")
    z, x = v // SIDE, v % SIDE
    y, c = w // 2, w % 2
    columns = head.shape[0]

    def at(dz, dx):
        return (lax.rem(z + dz + SIDE, SIDE) * SIDE + lax.rem(x + dx + SIDE, SIDE), w)

    def up(dy, other=0):
        return (v, lax.rem(y + dy + SIDE, SIDE) * 2 + (1 - c if other else c))

    def group(d):
        return lax.rem(w + d, GROUPS)

    def remote(src, dst, send, recv, dev):
        return pltpu.make_async_remote_copy(src_ref=src, dst_ref=dst, send_sem=send, recv_sem=recv,
                                            device_id=dev, device_id_type=MESH)

    barrier = pltpu.get_barrier_semaphore()
    peers = [(v, group(d)) for d in range(1, GROUPS)] + [at(0, 1), at(0, -1), at(1, 0), at(-1, 0)]
    for dev in peers:
        pl.semaphore_signal(barrier, inc=1, device_id=dev, device_id_type=MESH)
    own_gain = pltpu.make_async_copy(gain, gain_v, gs.at[0])
    own_ids = pltpu.make_async_copy(ids, ids_v, is_.at[0])
    lens_copy = pltpu.make_async_copy(lens, lens_v, ls_.at[0])
    for copy in (own_gain, own_ids, lens_copy):
        copy.start()
    for copy in (own_gain, own_ids, lens_copy):
        copy.wait()
    for g in range(GROUPS):
        for k in (0, 1):
            aux_tx[g, k:k + 1, :] = ids_v[k, g].astype(jnp.float32)
        aux_tx[g, 2:3, :] = gain_v[...]
    pl.semaphore_wait(barrier, len(peers))

    sent = []

    def go(copy):
        copy.start()
        sent.append(copy)

    a_copies, g_copies = {0: [], 1: []}, []
    own = []
    for h in (0, 1):
        for d in range(GROUPS):
            g = group(d)
            rows = pl.ds(pl.multiple_of(g * ROWS + h * HALF, HALF), HALF)
            place = xin.at[w, pl.ds(h * HALF, HALF), :]
            if d == 0:
                own.append(pltpu.make_async_copy(hid.at[rows, :], place, as_.at[h, 0]))
            else:
                a_copies[h].append(remote(hid.at[rows, :], place, as_.at[h, d], ar.at[h, d], (v, g)))
    for d in range(1, GROUPS):
        g = group(d)
        g_copies.append(remote(aux_tx.at[g], aux.at[w], gs.at[d], gr.at[d], (v, g)))
    def wcols(dy):
        src = lax.rem(y - dy + SIDE, SIDE) * 2 + c
        return pl.ds(pl.multiple_of(src * 128, 128), 128)

    W = {}
    wlocal = {}
    for j in range(NPART):
        n = min(PART, columns - j * PART)
        mine = head.at[pl.ds(j * PART, n), :]
        mid = PART // 2
        row0 = j % 2 * PART

        def wv(dy, lo=0, hi=n):
            return wb.at[j // 2, pl.ds(row0 + lo, hi - lo), wcols(dy)]

        def wcopy(k, src, dst, dev):
            W[j, k] = remote(src, dst, ws.at[j * 9 + k], wr.at[j * 9 + k], dev)

        wcopy(0, mine, wv(0), up(1))
        wcopy(1, mine, wv(0), up(-1))
        wcopy(2, mine, wv(0), up(0, 1))
        wcopy(3, wv(1, 0, mid), wv(1, 0, mid), up(1))
        wcopy(4, wv(1), wv(1), up(0, 1))
        wcopy(5, wv(3, mid), wv(3, mid), up(-1))
        wcopy(6, wv(3), wv(3), up(0, 1))
        wcopy(7, wv(2, 0, mid), wv(2, 0, mid), up(0, 1))
        wcopy(8, wv(2, mid), wv(2, mid), up(0, 1))
        wlocal[j] = pltpu.make_async_copy(mine, wv(0), wl.at[j])

    def w_own(j):
        for k in (0, 1, 2):
            go(W[j, k])
        wlocal[j].start()

    def w_forward(j):
        W[j, 0].wait_recv()
        go(W[j, 3])
        W[j, 1].wait_recv()
        go(W[j, 5])
        go(W[j, 4])
        go(W[j, 6])

    def w_across(j):
        W[j, 3].wait_recv()
        go(W[j, 7])
        W[j, 5].wait_recv()
        go(W[j, 8])

    def w_done(chunk):
        for j in (2 * chunk, 2 * chunk + 1):
            wlocal[j].wait()
            for k in (2, 4, 6, 7, 8):
                W[j, k].wait_recv()

    X = {}

    def turn(h, a, b):
        return (b, a) if h == 0 else (a, b)

    def xcopy(name, h, d, lo, n, step):
        to = ((d[0] + step[0]) % SIDE, (d[1] + step[1]) % SIDE)
        k = len(X)
        X[name] = remote(xn.at[PLACE[h, *d], pl.ds(lo, n), :], xn.at[PLACE[h, *to], pl.ds(lo, n), :],
                         xs.at[k], xr.at[k], at(*step))

    for h in (0, 1):
        for sgn, near in ((1, 1), (-1, 3)):
            q = 0 if sgn == 1 else 32
            xcopy((h, "first", near), h, (0, 0), 0, 64, turn(h, sgn, 0))
            xcopy((h, "first", 2, near), h, turn(h, near, 0), q, 32, turn(h, sgn, 0))
            for far in range(SIDE):
                xcopy((h, "second", far, near), h, turn(h, far, 0), 0, 64, turn(h, 0, sgn))
                xcopy((h, "last", far, near), h, turn(h, far, near), q, 32, turn(h, 0, sgn))

    def x_own(h):
        for near in (1, 3):
            go(X[h, "first", near])

    def x_own_across():
        for h in (0, 1):
            for near in (1, 3):
                go(X[h, "second", 0, near])

    def x_round1():
        for h in (0, 1):
            for near in (1, 3):
                X[h, "first", near].wait_recv()
                go(X[h, "first", 2, near])

    def x_near(near):
        for h in (0, 1):
            for side in (1, 3):
                go(X[h, "second", near, side])

    def x_pace():
        for h in (0, 1):
            for near in (1, 3):
                X[h, "second", 0, near].wait_recv()

    def x_round2():
        for h in (0, 1):
            for near in (1, 3):
                go(X[h, "last", 0, near])

    def x_round3_wait():
        for h in (0, 1):
            for near in (1, 3):
                X[h, "first", 2, near].wait_recv()

    def x_round3():
        for h in (0, 1):
            for side in (1, 3):
                go(X[h, "second", 2, side])

    def x_round4(far):
        for h in (0, 1):
            for near in (1, 3):
                X[h, "second", far, near].wait_recv()
                go(X[h, "last", far, near])

    def x_round5():
        for h in (0, 1):
            for near in (1, 3):
                X[h, "second", 2, near].wait_recv()
                go(X[h, "last", 2, near])

    def x_last(far):
        for h in (0, 1):
            for near in (1, 3):
                X[h, "last", far, near].wait_recv()

    far_first = (3, 4, 2, 5, 1, 6, 0)
    for copy in g_copies:
        go(copy)
    for k in far_first:
        go(a_copies[0][k])
    w_own(0)
    for k in far_first:
        go(a_copies[1][k])
    w_own(1)
    for copy in own:
        copy.start()
    aux[w] = aux_tx[w]

    m[...] = jnp.full(m.shape, NEG, jnp.float32)
    for ref in (s, u, t):
        ref[...] = jnp.zeros(ref.shape, jnp.float32)

    w_forward(0)
    w_own(2)

    for h in (0, 1):
        own[h].wait()
        for copy in a_copies[h]:
            copy.wait_recv()
        if h == 0:
            for copy in g_copies:
                copy.wait_recv()
        for r in range(0, HALF, 32):
            wide = [xin[k, h * HALF + r:h * HALF + r + 32, :].astype(jnp.float32) for k in range(GROUPS)]
            squares = wide[0] * wide[0]
            for k in range(1, GROUPS):
                squares = squares + wide[k] * wide[k]
            scale = lax.rsqrt(jnp.sum(squares, axis=1, keepdims=True) / D + 1e-06)
            for k in range(GROUPS):
                xn[h, r:r + 32, k * 128:(k + 1) * 128] = (wide[k] * scale * aux[k, 2:3, :]).astype(jnp.bfloat16)
        x_own(h)
        if h == 0:
            w_own(3)

    w_across(0)
    x_own_across()

    which = lax.broadcasted_iota(jnp.int32, (1, SEQS), 1) == v // 2
    limit = jnp.sum(jnp.where(which, lens_v[...], 0), axis=1, keepdims=True)

    lane = lax.broadcasted_iota(jnp.int32, (ROWS, 128), 1)
    base = v * columns
    for dz in range(SIDE):
        for dx in range(SIDE):
            block = lax.rem(z - dz + SIDE, SIDE) * SIDE + lax.rem(x - dx + SIDE, SIDE)
            row = aux[block // 2, pl.ds(block % 2, 1), :].astype(jnp.int32)
            row = jnp.where(row - base < columns, row - base, -1)
            wide = jnp.broadcast_to(row, (ROWS, 128)).T - lane
            for h in (0, 1):
                idl[PLACE[h, dz, dx]] = wide[h * HALF:(h + 1) * HALF, :]

    w_forward(1)
    w_own(4)
    w_forward(2)
    x_round1()
    x_near(1)
    w_forward(3)
    w_own(5)
    w_across(1)
    w_own(6)
    w_done(0)

    def pick(values, i):
        out = jnp.int32(values[0])
        for k in range(1, len(values)):
            if values[k] != values[k - 1]:
                out = jnp.where(i >= k, jnp.int32(values[k]), out)
        return out

    def tile_of(i):
        return pick([p for p, _ in STEPS], i), pick([j for _, j in STEPS], i)

    def dot(i, buf):
        p, j = tile_of(i)
        lhs = xn[pl.ds(p * 4, 4)].reshape(TILE, D)
        buf[...] = lax.dot_general(lhs, wb[j], (((1,), (1,)), ((), ())), preferred_element_type=jnp.float32)

    group_rows = 16
    parts = CHUNK // 128
    lane_g = lax.broadcasted_iota(jnp.int32, (group_rows, 128), 1)

    def stats(i, buf):
        p, j = tile_of(i)
        col0 = j * CHUNK
        edge = lane_g < columns - (parts - 1) * 128 - col0
        for g in range(TILE // group_rows):
            at_rows = (p * 4 + g * group_rows // HALF, pl.ds(g * group_rows % HALF, group_rows))
            ls = [buf[g * group_rows:(g + 1) * group_rows, k * 128:(k + 1) * 128] for k in range(parts)]
            ls[-1] = jnp.where(edge, ls[-1], NEG)
            m_old = m[at_rows]
            top = jnp.maximum(jnp.maximum(ls[0], ls[1]), jnp.maximum(ls[2], ls[3]))
            m_new = jnp.maximum(m_old, top)
            fade = jnp.exp(m_old - m_new)
            s_new = s[at_rows] * fade
            u_new = u[at_rows] * fade
            t_new = t[at_rows]
            here = idl[at_rows]
            for k in range(parts):
                e = jnp.exp(ls[k] - m_new)
                s_new = s_new + e
                u_new = u_new + e * ls[k]
                t_new = jnp.where(here == col0 + k * 128, ls[k], t_new)
            m[at_rows] = m_new
            s[at_rows] = s_new
            u[at_rows] = u_new
            t[at_rows] = t_new

    def finish(q, place=None):
        place = q if place is None else place

        def rows_of(ref):
            return ref[pl.ds(q * 2, 2)].reshape(ROWS, 128).T

        mt = rows_of(m)
        peak = jnp.max(mt, axis=0, keepdims=True)
        scale = jnp.exp(mt - peak)
        st_tx[place, 0:1, :] = peak
        st_tx[place, 1:2, :] = jnp.sum(rows_of(s) * scale, axis=0, keepdims=True)
        st_tx[place, 2:3, :] = jnp.sum(rows_of(u) * scale, axis=0, keepdims=True)
        st_tx[place, 3:4, :] = jnp.sum(rows_of(t), axis=0, keepdims=True)

    S = {}
    for k, (h, dz, dx) in enumerate(UNITS):
        if k >= 2 and not (k % 2 == 1 and UNITS[k - 1][1:] == (dz, dx)):
            S[k] = remote(st_tx.at[k // 2], st_rx.at[k], ss_.at[k], sr.at[k], at(-dz, -dx))

    def send_stats(tile):
        for k in range(tile * 4, tile * 4 + 4):
            if k in S:
                go(S[k])

    def finish_tile(tile):
        finish(tile * 2)
        finish(tile * 2 + 1)
        send_stats(tile)

    def acts_0():
        w_forward(4)
        w_own(7)
        w_across(2)
        x_near(3)
        w_across(3)
        x_pace()
        x_round2()
        x_round3_wait()
        x_round3()

    def acts_1():
        w_forward(5)
        w_forward(6)
        w_across(4)
        w_done(1)

    def acts_2():
        w_forward(7)
        w_across(5)
        x_round4(1)

    def acts_3():
        w_across(6)
        w_done(2)

    def acts_4():
        x_round4(3)

    def acts_5():
        w_across(7)

    def acts_7():
        x_round5()
        w_done(3)
        x_last(0)

    def acts_9():
        send_stats(4)
        x_last(1)

    def acts_11():
        send_stats(5)
        x_last(3)
        x_last(2)

    def acts_13():
        send_stats(6)

    EARLY = {0: acts_0, 1: acts_1, 2: acts_2, 3: acts_3, 4: acts_4, 5: acts_5, 7: acts_7}
    LATE = {9: acts_9, 11: acts_11, 13: acts_13}
    READY = [4, 8, 5, 8, 6, 8, 7]
    total = len(STEPS)
    dot(0, lb0)

    def block(h):
        i = h * 2
        dot(i + 1, lb1)
        stats(i, lb0)
        dot(jnp.minimum(i + 2, total - 1), lb0)
        stats(i + 1, lb1)

    @pl.loop(0, 8)
    def _(h):
        for k in EARLY:
            pl.when(h == k)(EARLY[k])
        block(h)

    @pl.loop(8, total // 2 - 1)
    def _(h):
        for k in LATE:
            pl.when(h == k)(LATE[k])
        place = pick(READY, h - 8) * 2
        source = jnp.minimum(place, 14)
        finish(source, place)
        finish(source + 1, place + 1)
        block(h)

    send_stats(7)
    for q in (6, 7, 4, 5):
        finish(q)
    block(total // 2 - 1)
    send_stats(3)
    send_stats(2)
    for tile in (1, 0):
        finish_tile(tile)
    for copy in S.values():
        copy.wait_recv()

    first_half = lax.broadcasted_iota(jnp.int32, (4, 128), 1) < HALF

    def stat_of(dz, dx):
        if (dz, dx) == (0, 0):
            return st_tx[0]
        a, b = PLACE[0, dz, dx], PLACE[1, dz, dx]
        if b not in S:
            return st_rx[a]
        return jnp.where(first_half, st_rx[a], st_rx[b])

    stat = [stat_of(dz, dx) for dz in range(SIDE) for dx in range(SIDE)]
    peak = stat[0][0:1, :]
    for a in stat[1:]:
        peak = jnp.maximum(peak, a[0:1, :])
    sum_e = jnp.zeros_like(peak)
    sum_w = jnp.zeros_like(peak)
    target = jnp.zeros_like(peak)
    for a in stat:
        f = jnp.exp(a[0:1, :] - peak)
        sum_e = sum_e + a[1:2, :] * f
        sum_w = sum_w + a[2:3, :] * f
        target = target + a[3:4, :]
    log_total = peak + jnp.log(sum_e)
    position = lax.rem(v, 2) * (SEQ_LEN // 2) + w * ROWS + lax.broadcasted_iota(jnp.int32, (1, 128), 1)
    live = position < limit
    o_tx[0] = jnp.where(live, target - log_total, 0.0)
    o_tx[1] = jnp.where(live, log_total - sum_w / sum_e, 0.0)

    goal = v // 2
    mine = lax.rem(v, 2) * GROUPS + w

    def result(k, place, dev):
        return remote(o_tx, out.at[:, place], os_.at[k], or_.at[place], dev)

    o_own = pltpu.make_async_copy(o_tx, out.at[:, mine], os_.at[16])
    for k in range(16):
        @pl.when(jnp.logical_not(jnp.logical_and(k == v, goal == w)))
        def _():
            result(k, mine, (k, goal)).start()

    @pl.when(goal == w)
    def _():
        o_own.start()

    for copy in sent:
        copy.wait_send()
    for k in range(16):
        @pl.when(jnp.logical_not(jnp.logical_and(2 * w + k // GROUPS == v, k % GROUPS == w)))
        def _():
            result(k, k, (v, w)).wait_recv()

        @pl.when(jnp.logical_not(jnp.logical_and(k == v, goal == w)))
        def _():
            result(k, mine, (k, goal)).wait_send()

    @pl.when(goal == w)
    def _():
        o_own.wait()


def on_device(hidden, norm_gain, head_weight, token_ids, seq_lengths):
    hbm = pl.BlockSpec(memory_space=pl.ANY)
    f32, bf16, i32 = jnp.float32, jnp.bfloat16, jnp.int32
    dma = pltpu.SemaphoreType.DMA
    rows = pltpu.VMEM((32, HALF, 128), f32)
    scores = pl.pallas_call(
        kernel,
        out_shape=jax.ShapeDtypeStruct((2, 16, 1, 128), f32),
        in_specs=[hbm, hbm, hbm, hbm, hbm],
        out_specs=hbm,
        scratch_shapes=[
            pltpu.VMEM((GROUPS, ROWS, 128), bf16),
            pltpu.VMEM((32, HALF, D), bf16),
            pltpu.VMEM((NCHUNK, CHUNK, D), bf16),
            pltpu.VMEM((GROUPS, 3, 128), f32),
            pltpu.VMEM((32, HALF, 128), i32),
            rows, rows, rows, rows,
            pltpu.VMEM((TILE, CHUNK), f32),
            pltpu.VMEM((TILE, CHUNK), f32),
            pltpu.VMEM((18, 4, 128), f32),
            pltpu.VMEM((32, 4, 128), f32),
            pltpu.VMEM((2, 1, 128), f32),
            pltpu.VMEM((1, SEQS), i32),
            pltpu.VMEM((1, 128), f32),
            pltpu.VMEM((2, GROUPS, 1, 128), i32),
            pltpu.VMEM((GROUPS, 3, 128), f32),
            dma((2, 8)), dma((2, 8)), dma((8,)), dma((8,)), dma((1,)),
            dma((40,)), dma((40,)), dma((72,)), dma((72,)), dma((8,)),
            dma((32,)), dma((32,)), dma((17,)), dma((16,)), dma((1,)),
        ],
        compiler_params=pltpu.CompilerParams(
            collective_id=0, has_side_effects=True, vmem_limit_bytes=56 * 2**20),
        name="score",
    )(hidden, head_weight.T, norm_gain.reshape(1, 128), token_ids.reshape(2, GROUPS, 1, 128),
      seq_lengths.reshape(1, SEQS))
    return scores[0].reshape(SEQ_LEN), scores[1].reshape(SEQ_LEN)


def solution(mesh):
    in_specs = (P("vocab", "width"), P("width"), P("width", "vocab"), P("width"), P())
    out_specs = (P("width"), P("width"))
    return jax.shard_map(
        on_device, mesh=mesh, in_specs=in_specs, out_specs=out_specs, check_vma=False
    )
```

```python
import jax
import jax.numpy as jnp
from jax import lax
from jax.experimental import pallas as pl
from jax.experimental.pallas import tpu as pltpu
from jax.sharding import PartitionSpec as P

D = 1024
SEQ_LEN = 2048
SEQS = 8
SIDE = 4
GROUPS = 8
ROWS = 128
HALF = 64
CHUNK = 512
NCHUNK = 4
TILE = 256
NEG = -1e30
MESH = pl.DeviceIdType.MESH
UNITS = [(0, 0, 0), (1, 0, 0), (0, 0, 1), (1, 1, 0),
         (0, 0, 3), (1, 3, 0), (0, 1, 0), (1, 0, 1),
         (0, 3, 0), (1, 0, 3), (0, 0, 2), (1, 2, 0),
         (0, 1, 1), (1, 1, 1), (0, 3, 1), (1, 1, 3),
         (0, 1, 3), (1, 3, 1), (0, 3, 3), (1, 3, 3),
         (0, 2, 0), (1, 0, 2), (0, 1, 2), (1, 2, 1),
         (0, 3, 2), (1, 2, 3), (0, 2, 1), (1, 1, 2),
         (0, 2, 3), (1, 3, 2), (0, 2, 2), (1, 2, 2)]
PLACE = {d: i for i, d in enumerate(UNITS)}
NTILE = 8
STEPS = [(0, 0), (1, 0), (2, 0), (0, 1), (1, 1), (2, 1), (3, 0), (3, 1),
         (0, 2), (1, 2), (2, 2), (3, 2), (4, 0), (4, 1), (4, 2), (4, 3),
         (5, 0), (5, 1), (5, 2), (5, 3), (6, 0), (6, 1), (6, 2), (6, 3),
         (7, 0), (7, 1), (7, 2), (7, 3), (3, 3), (2, 3), (1, 3), (0, 3)]
PART = 256
NPART = 8


def kernel(hid, head, gain, ids, lens, out,
           xin, xn, wb, aux, idl, m, s, u, t, lb0, lb1, st_tx, st_rx, o_tx, lens_v, gain_v, ids_v, aux_tx,
           as_, ar, gs, gr, is_, xs, xr, ws, wr, wl, ss_, sr, os_, or_, ls_):
    v = lax.axis_index("vocab")
    w = lax.axis_index("width")
    z, x = v // SIDE, v % SIDE
    y, c = w // 2, w % 2
    columns = head.shape[0]

    def at(dz, dx):
        return (lax.rem(z + dz + SIDE, SIDE) * SIDE + lax.rem(x + dx + SIDE, SIDE), w)

    def up(dy, other=0):
        return (v, lax.rem(y + dy + SIDE, SIDE) * 2 + (1 - c if other else c))

    def group(d):
        return lax.rem(w + d, GROUPS)

    def remote(src, dst, send, recv, dev):
        return pltpu.make_async_remote_copy(src_ref=src, dst_ref=dst, send_sem=send, recv_sem=recv,
                                            device_id=dev, device_id_type=MESH)

    barrier = pltpu.get_barrier_semaphore()
    peers = [(v, group(d)) for d in range(1, GROUPS)] + [at(0, 1), at(0, -1), at(1, 0), at(-1, 0)]
    for dev in peers:
        pl.semaphore_signal(barrier, inc=1, device_id=dev, device_id_type=MESH)
    own_gain = pltpu.make_async_copy(gain, gain_v, gs.at[0])
    own_ids = pltpu.make_async_copy(ids, ids_v, is_.at[0])
    lens_copy = pltpu.make_async_copy(lens, lens_v, ls_.at[0])
    for copy in (own_gain, own_ids, lens_copy):
        copy.start()
    for copy in (own_gain, own_ids, lens_copy):
        copy.wait()
    for g in range(GROUPS):
        for k in (0, 1):
            aux_tx[g, k:k + 1, :] = ids_v[k, g].astype(jnp.float32)
        aux_tx[g, 2:3, :] = gain_v[...]
    pl.semaphore_wait(barrier, len(peers))

    sent = []

    def go(copy):
        copy.start()
        sent.append(copy)

    a_copies, g_copies = {0: [], 1: []}, []
    own = []
    for h in (0, 1):
        for d in range(GROUPS):
            g = group(d)
            rows = pl.ds(pl.multiple_of(g * ROWS + h * HALF, HALF), HALF)
            place = xin.at[w, pl.ds(h * HALF, HALF), :]
            if d == 0:
                own.append(pltpu.make_async_copy(hid.at[rows, :], place, as_.at[h, 0]))
            else:
                a_copies[h].append(remote(hid.at[rows, :], place, as_.at[h, d], ar.at[h, d], (v, g)))
    for d in range(1, GROUPS):
        g = group(d)
        g_copies.append(remote(aux_tx.at[g], aux.at[w], gs.at[d], gr.at[d], (v, g)))
    def wcols(dy):
        src = lax.rem(y - dy + SIDE, SIDE) * 2 + c
        return pl.ds(pl.multiple_of(src * 128, 128), 128)

    W = {}
    wlocal = {}
    for j in range(NPART):
        n = min(PART, columns - j * PART)
        mine = head.at[pl.ds(j * PART, n), :]
        mid = PART // 2
        row0 = j % 2 * PART

        def wv(dy, lo=0, hi=n):
            return wb.at[j // 2, pl.ds(row0 + lo, hi - lo), wcols(dy)]

        def wcopy(k, src, dst, dev):
            W[j, k] = remote(src, dst, ws.at[j * 9 + k], wr.at[j * 9 + k], dev)

        wcopy(0, mine, wv(0), up(1))
        wcopy(1, mine, wv(0), up(-1))
        wcopy(2, mine, wv(0), up(0, 1))
        wcopy(3, wv(1, 0, mid), wv(1, 0, mid), up(1))
        wcopy(4, wv(1), wv(1), up(0, 1))
        wcopy(5, wv(3, mid), wv(3, mid), up(-1))
        wcopy(6, wv(3), wv(3), up(0, 1))
        wcopy(7, wv(2, 0, mid), wv(2, 0, mid), up(0, 1))
        wcopy(8, wv(2, mid), wv(2, mid), up(0, 1))
        wlocal[j] = pltpu.make_async_copy(mine, wv(0), wl.at[j])

    def w_own(j):
        for k in (0, 1, 2):
            go(W[j, k])
        wlocal[j].start()

    def w_forward(j):
        W[j, 0].wait_recv()
        go(W[j, 3])
        W[j, 1].wait_recv()
        go(W[j, 5])
        go(W[j, 4])
        go(W[j, 6])

    def w_across(j):
        W[j, 3].wait_recv()
        go(W[j, 7])
        W[j, 5].wait_recv()
        go(W[j, 8])

    def w_done(chunk):
        for j in (2 * chunk, 2 * chunk + 1):
            wlocal[j].wait()
            for k in (2, 4, 6, 7, 8):
                W[j, k].wait_recv()

    X = {}

    def turn(h, a, b):
        return (b, a) if h == 0 else (a, b)

    def xcopy(name, h, d, lo, n, step):
        to = ((d[0] + step[0]) % SIDE, (d[1] + step[1]) % SIDE)
        k = len(X)
        X[name] = remote(xn.at[PLACE[h, *d], pl.ds(lo, n), :], xn.at[PLACE[h, *to], pl.ds(lo, n), :],
                         xs.at[k], xr.at[k], at(*step))

    for h in (0, 1):
        for sgn, near in ((1, 1), (-1, 3)):
            q = 0 if sgn == 1 else 32
            xcopy((h, "first", near), h, (0, 0), 0, 64, turn(h, sgn, 0))
            xcopy((h, "first", 2, near), h, turn(h, near, 0), q, 32, turn(h, sgn, 0))
            for far in range(SIDE):
                xcopy((h, "second", far, near), h, turn(h, far, 0), 0, 64, turn(h, 0, sgn))
                xcopy((h, "last", far, near), h, turn(h, far, near), q, 32, turn(h, 0, sgn))

    def x_own(h):
        for near in (1, 3):
            go(X[h, "first", near])

    def x_own_across():
        for h in (0, 1):
            for near in (1, 3):
                go(X[h, "second", 0, near])

    def x_round1():
        for h in (0, 1):
            for near in (1, 3):
                X[h, "first", near].wait_recv()
                go(X[h, "first", 2, near])

    def x_near(near):
        for h in (0, 1):
            for side in (1, 3):
                go(X[h, "second", near, side])

    def x_pace():
        for h in (0, 1):
            for near in (1, 3):
                X[h, "second", 0, near].wait_recv()

    def x_round2():
        for h in (0, 1):
            for near in (1, 3):
                go(X[h, "last", 0, near])

    def x_round3_wait():
        for h in (0, 1):
            for near in (1, 3):
                X[h, "first", 2, near].wait_recv()

    def x_round3():
        for h in (0, 1):
            for side in (1, 3):
                go(X[h, "second", 2, side])

    def x_round4(far):
        for h in (0, 1):
            for near in (1, 3):
                X[h, "second", far, near].wait_recv()
                go(X[h, "last", far, near])

    def x_round5():
        for h in (0, 1):
            for near in (1, 3):
                X[h, "second", 2, near].wait_recv()
                go(X[h, "last", 2, near])

    def x_last(far):
        for h in (0, 1):
            for near in (1, 3):
                X[h, "last", far, near].wait_recv()

    far_first = (3, 4, 2, 5, 1, 6, 0)
    for copy in g_copies:
        go(copy)
    for k in far_first:
        go(a_copies[0][k])
    w_own(0)
    for k in far_first:
        go(a_copies[1][k])
    w_own(1)
    for copy in own:
        copy.start()
    aux[w] = aux_tx[w]

    m[...] = jnp.full(m.shape, NEG, jnp.float32)
    for ref in (s, u, t):
        ref[...] = jnp.zeros(ref.shape, jnp.float32)

    w_forward(0)
    w_own(2)

    for h in (0, 1):
        own[h].wait()
        for copy in a_copies[h]:
            copy.wait_recv()
        if h == 0:
            for copy in g_copies:
                copy.wait_recv()
        for r in range(0, HALF, 32):
            wide = [xin[k, h * HALF + r:h * HALF + r + 32, :].astype(jnp.float32) for k in range(GROUPS)]
            squares = wide[0] * wide[0]
            for k in range(1, GROUPS):
                squares = squares + wide[k] * wide[k]
            scale = lax.rsqrt(jnp.sum(squares, axis=1, keepdims=True) / D + 1e-06)
            for k in range(GROUPS):
                xn[h, r:r + 32, k * 128:(k + 1) * 128] = (wide[k] * scale * aux[k, 2:3, :]).astype(jnp.bfloat16)
        x_own(h)
        if h == 0:
            w_own(3)

    x_own_across()
    w_across(0)

    which = lax.broadcasted_iota(jnp.int32, (1, SEQS), 1) == v // 2
    limit = jnp.sum(jnp.where(which, lens_v[...], 0), axis=1, keepdims=True)

    lane = lax.broadcasted_iota(jnp.int32, (ROWS, 128), 1)
    base = v * columns
    for dz in range(SIDE):
        for dx in range(SIDE):
            block = lax.rem(z - dz + SIDE, SIDE) * SIDE + lax.rem(x - dx + SIDE, SIDE)
            row = aux[block // 2, pl.ds(block % 2, 1), :].astype(jnp.int32)
            row = jnp.where(row - base < columns, row - base, -1)
            wide = jnp.broadcast_to(row, (ROWS, 128)).T - lane
            for h in (0, 1):
                idl[PLACE[h, dz, dx]] = wide[h * HALF:(h + 1) * HALF, :]

    w_forward(1)
    w_own(4)
    w_forward(2)
    x_round1()
    x_near(1)
    w_forward(3)
    w_own(5)
    w_across(1)
    w_own(6)
    w_done(0)

    def pick(values, i):
        out = jnp.int32(values[0])
        for k in range(1, len(values)):
            if values[k] != values[k - 1]:
                out = jnp.where(i >= k, jnp.int32(values[k]), out)
        return out

    def tile_of(i):
        return pick([p for p, _ in STEPS], i), pick([j for _, j in STEPS], i)

    def dot(i, buf):
        p, j = tile_of(i)
        lhs = xn[pl.ds(p * 4, 4)].reshape(TILE, D)
        buf[...] = lax.dot_general(lhs, wb[j], (((1,), (1,)), ((), ())), preferred_element_type=jnp.float32)

    group_rows = 16
    parts = CHUNK // 128
    lane_g = lax.broadcasted_iota(jnp.int32, (group_rows, 128), 1)

    def stats(i, buf):
        p, j = tile_of(i)
        col0 = j * CHUNK
        edge = lane_g < columns - (parts - 1) * 128 - col0
        for g in range(TILE // group_rows):
            at_rows = (p * 4 + g * group_rows // HALF, pl.ds(g * group_rows % HALF, group_rows))
            ls = [buf[g * group_rows:(g + 1) * group_rows, k * 128:(k + 1) * 128] for k in range(parts)]
            ls[-1] = jnp.where(edge, ls[-1], NEG)
            m_old = m[at_rows]
            top = jnp.maximum(jnp.maximum(ls[0], ls[1]), jnp.maximum(ls[2], ls[3]))
            m_new = jnp.maximum(m_old, top)
            fade = jnp.exp(m_old - m_new)
            s_new = s[at_rows] * fade
            u_new = u[at_rows] * fade
            t_new = t[at_rows]
            here = idl[at_rows]
            for k in range(parts):
                e = jnp.exp(ls[k] - m_new)
                s_new = s_new + e
                u_new = u_new + e * ls[k]
                t_new = jnp.where(here == col0 + k * 128, ls[k], t_new)
            m[at_rows] = m_new
            s[at_rows] = s_new
            u[at_rows] = u_new
            t[at_rows] = t_new

    def finish(q, place=None):
        place = q if place is None else place

        def rows_of(ref):
            return ref[pl.ds(q * 2, 2)].reshape(ROWS, 128).T

        mt = rows_of(m)
        peak = jnp.max(mt, axis=0, keepdims=True)
        scale = jnp.exp(mt - peak)
        st_tx[place, 0:1, :] = peak
        st_tx[place, 1:2, :] = jnp.sum(rows_of(s) * scale, axis=0, keepdims=True)
        st_tx[place, 2:3, :] = jnp.sum(rows_of(u) * scale, axis=0, keepdims=True)
        st_tx[place, 3:4, :] = jnp.sum(rows_of(t), axis=0, keepdims=True)

    S = {}
    for k, (h, dz, dx) in enumerate(UNITS):
        if k >= 2 and not (k % 2 == 1 and UNITS[k - 1][1:] == (dz, dx)):
            S[k] = remote(st_tx.at[k // 2], st_rx.at[k], ss_.at[k], sr.at[k], at(-dz, -dx))

    def send_stats(tile):
        for k in range(tile * 4, tile * 4 + 4):
            if k in S:
                go(S[k])

    def finish_tile(tile):
        finish(tile * 2)
        finish(tile * 2 + 1)
        send_stats(tile)

    def acts_0():
        w_forward(4)
        w_own(7)
        w_across(2)
        x_near(3)
        w_across(3)
        x_pace()
        x_round2()
        x_round3_wait()
        x_round3()

    def acts_1():
        w_forward(5)
        w_forward(6)
        w_across(4)
        w_done(1)

    def acts_2():
        w_forward(7)
        w_across(5)
        x_round4(1)

    def acts_3():
        w_across(6)
        w_done(2)

    def acts_4():
        x_round4(3)

    def acts_5():
        w_across(7)

    def acts_7():
        x_round5()
        w_done(3)
        x_last(0)

    def acts_9():
        send_stats(4)
        x_last(1)

    def acts_11():
        send_stats(5)
        x_last(3)
        x_last(2)

    def acts_13():
        send_stats(6)

    EARLY = {0: acts_0, 1: acts_1, 2: acts_2, 3: acts_3, 4: acts_4, 5: acts_5, 7: acts_7}
    LATE = {9: acts_9, 11: acts_11, 13: acts_13}
    READY = [4, 8, 5, 8, 6, 8, 7]
    total = len(STEPS)
    dot(0, lb0)

    def block(h):
        i = h * 2
        dot(i + 1, lb1)
        stats(i, lb0)
        dot(jnp.minimum(i + 2, total - 1), lb0)
        stats(i + 1, lb1)

    @pl.loop(0, 8)
    def _(h):
        for k in EARLY:
            pl.when(h == k)(EARLY[k])
        block(h)

    @pl.loop(8, total // 2 - 1)
    def _(h):
        for k in LATE:
            pl.when(h == k)(LATE[k])
        place = pick(READY, h - 8) * 2
        source = jnp.minimum(place, 14)
        finish(source, place)
        finish(source + 1, place + 1)
        block(h)

    send_stats(7)
    for q in (6, 7, 4, 5):
        finish(q)
    block(total // 2 - 1)
    send_stats(3)
    send_stats(2)
    for tile in (1, 0):
        finish_tile(tile)
    for copy in S.values():
        copy.wait_recv()

    first_half = lax.broadcasted_iota(jnp.int32, (4, 128), 1) < HALF

    def stat_of(dz, dx):
        if (dz, dx) == (0, 0):
            return st_tx[0]
        a, b = PLACE[0, dz, dx], PLACE[1, dz, dx]
        if b not in S:
            return st_rx[a]
        return jnp.where(first_half, st_rx[a], st_rx[b])

    stat = [stat_of(dz, dx) for dz in range(SIDE) for dx in range(SIDE)]
    peak = stat[0][0:1, :]
    for a in stat[1:]:
        peak = jnp.maximum(peak, a[0:1, :])
    sum_e = jnp.zeros_like(peak)
    sum_w = jnp.zeros_like(peak)
    target = jnp.zeros_like(peak)
    for a in stat:
        f = jnp.exp(a[0:1, :] - peak)
        sum_e = sum_e + a[1:2, :] * f
        sum_w = sum_w + a[2:3, :] * f
        target = target + a[3:4, :]
    log_total = peak + jnp.log(sum_e)
    position = lax.rem(v, 2) * (SEQ_LEN // 2) + w * ROWS + lax.broadcasted_iota(jnp.int32, (1, 128), 1)
    live = position < limit
    o_tx[0] = jnp.where(live, target - log_total, 0.0)
    o_tx[1] = jnp.where(live, log_total - sum_w / sum_e, 0.0)

    goal = v // 2
    mine = lax.rem(v, 2) * GROUPS + w

    def result(k, place, dev):
        return remote(o_tx, out.at[:, place], os_.at[k], or_.at[place], dev)

    o_own = pltpu.make_async_copy(o_tx, out.at[:, mine], os_.at[16])
    for k in range(16):
        @pl.when(jnp.logical_not(jnp.logical_and(k == v, goal == w)))
        def _():
            result(k, mine, (k, goal)).start()

    @pl.when(goal == w)
    def _():
        o_own.start()

    for copy in sent:
        copy.wait_send()
    for k in range(16):
        @pl.when(jnp.logical_not(jnp.logical_and(2 * w + k // GROUPS == v, k % GROUPS == w)))
        def _():
            result(k, k, (v, w)).wait_recv()

        @pl.when(jnp.logical_not(jnp.logical_and(k == v, goal == w)))
        def _():
            result(k, mine, (k, goal)).wait_send()

    @pl.when(goal == w)
    def _():
        o_own.wait()


def on_device(hidden, norm_gain, head_weight, token_ids, seq_lengths):
    hbm = pl.BlockSpec(memory_space=pl.ANY)
    f32, bf16, i32 = jnp.float32, jnp.bfloat16, jnp.int32
    dma = pltpu.SemaphoreType.DMA
    rows = pltpu.VMEM((32, HALF, 128), f32)
    scores = pl.pallas_call(
        kernel,
        out_shape=jax.ShapeDtypeStruct((2, 16, 1, 128), f32),
        in_specs=[hbm, hbm, hbm, hbm, hbm],
        out_specs=hbm,
        scratch_shapes=[
            pltpu.VMEM((GROUPS, ROWS, 128), bf16),
            pltpu.VMEM((32, HALF, D), bf16),
            pltpu.VMEM((NCHUNK, CHUNK, D), bf16),
            pltpu.VMEM((GROUPS, 3, 128), f32),
            pltpu.VMEM((32, HALF, 128), i32),
            rows, rows, rows, rows,
            pltpu.VMEM((TILE, CHUNK), f32),
            pltpu.VMEM((TILE, CHUNK), f32),
            pltpu.VMEM((18, 4, 128), f32),
            pltpu.VMEM((32, 4, 128), f32),
            pltpu.VMEM((2, 1, 128), f32),
            pltpu.VMEM((1, SEQS), i32),
            pltpu.VMEM((1, 128), f32),
            pltpu.VMEM((2, GROUPS, 1, 128), i32),
            pltpu.VMEM((GROUPS, 3, 128), f32),
            dma((2, 8)), dma((2, 8)), dma((8,)), dma((8,)), dma((1,)),
            dma((40,)), dma((40,)), dma((72,)), dma((72,)), dma((8,)),
            dma((32,)), dma((32,)), dma((17,)), dma((16,)), dma((1,)),
        ],
        compiler_params=pltpu.CompilerParams(
            collective_id=0, has_side_effects=True, vmem_limit_bytes=56 * 2**20),
        name="score",
    )(hidden, head_weight.T, norm_gain.reshape(1, 128), token_ids.reshape(2, GROUPS, 1, 128),
      seq_lengths.reshape(1, SEQS))
    return scores[0].reshape(SEQ_LEN), scores[1].reshape(SEQ_LEN)


def solution(mesh):
    in_specs = (P("vocab", "width"), P("width"), P("width", "vocab"), P("width"), P())
    out_specs = (P("width"), P("width"))
    return jax.shard_map(
        on_device, mesh=mesh, in_specs=in_specs, out_specs=out_specs, check_vma=False
    )
```
